128 devices in a mesh: lon: 64 (over x, z, y_hi, core), lat: 2 (over y_lo).
Axes of the slice: x: 4, y: 4 (y_hi: 2, y_lo: 2; y = y_hi * 2 + y_lo), z: 4, core: 2. Of those that a mesh axis runs over, the one named last changes fastest.
Arguments:
- rows_in: bfloat16 [128, 4096, 256], P(('lat', 'lon')), may hold values from -6 to 6
- row_shift: int32 [128], P(('lat', 'lon')), may hold values from 0 to 4095, as said below
- kernel: float32 [9, 256], replicated, may hold values from -2 to 2
- w_in: bfloat16 [256, 1024], replicated, may hold values from -0.375 to 0.375
- w_out: bfloat16 [1024, 256], replicated, may hold values from -0.1875 to 0.1875
- cotangent: bfloat16 [128, 4096, 256], P('lat', 'lon'), may hold values from -6 to 6
Outputs:
- block_out: bfloat16 [128, 4096, 256], P('lat', 'lon')
- grad_rows: bfloat16 [128, 4096, 256], P(('lat', 'lon'))
- grad_kernel: float32 [9, 256], replicated
- grad_w_in: float32 [256, 1024], replicated
- grad_w_out: float32 [1024, 256], replicated
The draws below stay inside these ranges and needn't reach their ends.
Inputs may be any that keep to these rules, and one draw needn't show every extreme that they name: `row_shift`: some row has rotation 0 and some row has rotation 4096 - 1.
All inputs are finite; a program needn't handle non-finite values.
Results may differ from the reference program's by a relative error of at most 0.0065.
Values may be sent and summed in bfloat16 or wider, within the bound.
A program may use at most 128 MiB of HBM per device.

```python
import math
import jax
import jax.numpy as jnp
from jax import lax

C = 256
FF = 1024
NLAT = 128
NLON = 4096


def draw_row_shift(key, part):
    first, second = jax.random.split(jax.random.fold_in(key, 17))
    values = jax.random.randint(first, (NLAT,), 0, NLON)
    places = jax.random.permutation(second, NLAT)
    values = values.at[places[0]].set(0)
    values = values.at[places[1]].set(NLON - 1)
    return values.astype(jnp.int32)


def levels(own_key, shape, shards, least, high):
    level = 1.0
    for dim, shards_of in shards:
        draws = jax.random.uniform(jax.random.fold_in(jax.random.fold_in(own_key, 6), dim), (shards_of,), jnp.float32, least / len(shards), high / len(shards))
        level = level * jnp.repeat(jnp.exp(draws), shape[dim] // shards_of).reshape((-1,) + (1,) * (len(shape) - 1 - dim))
    return level


def normal_values(own_key, shape, scale, bound, shards=(), held_as=jnp.bfloat16):
    array = jax.random.normal(own_key, shape, jnp.float32) * scale
    if len(shards) > 0:
        array = levels(own_key, shape, shards, -0.22, 0.18) * array
    return jnp.clip(array, min=-bound, max=bound).astype(held_as)


def setup_inputs(seed: int = 0) -> dict:
    keys = jax.random.split(jax.random.key(seed), 7)
    rows_in = normal_values(keys[0], (NLAT, NLON, C), 1.0, 6.0, ((0, 128),))
    row_shift = draw_row_shift(jax.random.fold_in(keys[6], 71), 0)
    kernel = normal_values(keys[2], (9, C), 9 ** -0.5, 2.0, (), jnp.float32)
    w_in = normal_values(keys[3], (C, FF), C ** -0.5, 0.375)
    w_out = normal_values(keys[4], (FF, C), FF ** -0.5, 0.1875)
    cotangent = normal_values(keys[5], (NLAT, NLON, C), 1.0, 6.0, ((0, 2), (1, 64)))
    return {"rows_in": rows_in, "row_shift": row_shift, "kernel": kernel, "w_in": w_in, "w_out": w_out, "cotangent": cotangent}


GELU_C = math.sqrt(2.0 / math.pi)
TAPS = [(a, b) for a in (-1, 0, 1) for b in (-1, 0, 1)]

def gelu_value(h):
    inner = GELU_C * (h + 0.044715 * h * h * h)
    return 0.5 * h * (1.0 + jnp.tanh(inner))

def gelu_slope(h):
    t = jnp.tanh(GELU_C * (h + 0.044715 * h * h * h))
    return 0.5 * (1.0 + t) + 0.5 * h * (1.0 - t * t) * GELU_C * (1.0 + 3.0 * 0.044715 * h * h)

def wrap_pad(field):
    wide = jnp.concatenate([field[:, -4:], field, field[:, :4]], axis=1)
    return jnp.pad(wide, ((4, 4), (0, 0), (0, 0)))

def reference(rows_in, row_shift, kernel, w_in, w_out, cotangent):
    column = lax.broadcasted_iota(jnp.int32, (NLAT, NLON), 1)
    shifts = row_shift.astype(jnp.int32)[:, None]
    fwd_index = (column + shifts) % NLON
    band = jnp.take_along_axis(rows_in, fwd_index[:, :, None], axis=1)
    padded = wrap_pad(band).astype(jnp.float32)
    depth = jnp.zeros((NLAT, NLON, C), jnp.float32)
    for tap, (a, b) in enumerate(TAPS):
        depth = depth + kernel[tap] * padded[4 + 4 * a:4 + 4 * a + NLAT, 4 + 4 * b:4 + 4 * b + NLON]
    mean = lax.optimization_barrier(jnp.mean(depth, axis=-1, keepdims=True))
    centred = depth - mean
    rinv = lax.rsqrt(lax.optimization_barrier(jnp.mean(centred * centred, axis=-1, keepdims=True)) + 1e-06)
    nhat = centred * rinv
    normed = nhat.astype(jnp.bfloat16)

    def row_step(carry, items):
        grad_in, grad_out = carry
        normed_row, band_row, cot_row = items
        hidden = jnp.dot(normed_row, w_in, preferred_element_type=jnp.float32)
        act = gelu_value(hidden).astype(jnp.bfloat16)
        mlp_out = jnp.dot(act, w_out, preferred_element_type=jnp.float32)
        out_row = (band_row.astype(jnp.float32) + mlp_out).astype(jnp.bfloat16)
        g_act = jnp.dot(cot_row, w_out.T, preferred_element_type=jnp.float32)
        g_hidden = (g_act * gelu_slope(hidden)).astype(jnp.bfloat16)
        grad_out = grad_out + jnp.dot(act.T, cot_row, preferred_element_type=jnp.float32)
        grad_in = grad_in + jnp.dot(normed_row.T, g_hidden, preferred_element_type=jnp.float32)
        g_norm = jnp.dot(g_hidden, w_in.T, preferred_element_type=jnp.float32)
        return ((grad_in, grad_out), (out_row, g_norm))
    start = (jnp.zeros((C, FF), jnp.float32), jnp.zeros((FF, C), jnp.float32))
    (grad_in, grad_out), (block_out, g_norm) = lax.scan(row_step, start, (normed, band, cotangent))
    g_mean = lax.optimization_barrier(jnp.mean(g_norm, axis=-1, keepdims=True))
    g_proj = lax.optimization_barrier(jnp.mean(g_norm * nhat, axis=-1, keepdims=True))
    g_dw = (rinv * (g_norm - g_mean - nhat * g_proj)).astype(jnp.bfloat16)
    g_dw_wide = g_dw.astype(jnp.float32)
    scale = 1.0 / math.sqrt(NLAT * NLON)
    kernel_terms = []
    for tap, (a, b) in enumerate(TAPS):
        piece = padded[4 + 4 * a:4 + 4 * a + NLAT, 4 + 4 * b:4 + 4 * b + NLON]
        kernel_terms.append(lax.optimization_barrier(jnp.sum(piece * g_dw_wide, axis=(0, 1))))
    grad_kernel = scale * jnp.stack(kernel_terms)
    g_pad = wrap_pad(g_dw).astype(jnp.float32)
    g_band = cotangent.astype(jnp.float32)
    for tap, (a, b) in enumerate(TAPS):
        g_band = g_band + kernel[tap] * g_pad[4 - 4 * a:4 - 4 * a + NLAT, 4 - 4 * b:4 - 4 * b + NLON]
    back_index = (column - shifts) % NLON
    grad_rows = jnp.take_along_axis(g_band, back_index[:, :, None], axis=1).astype(jnp.bfloat16)
    return (block_out, grad_rows, grad_kernel, scale * grad_in, scale * grad_out)
```

```python
import functools
import math

import jax
import jax.numpy as jnp
from jax import lax
from jax.experimental import pallas as pl
from jax.experimental.pallas import tpu as pltpu
from jax.sharding import PartitionSpec as P

MESH = pl.DeviceIdType.MESH
GELU_C = math.sqrt(2.0 / math.pi)
GELU_A = 0.044715
EPS = 1e-06
F32 = jnp.float32
BF16 = jnp.bfloat16

NLON = 4096
C = 256
FF = 1024
DEVS = 64
CHAINS = 4
ROWS = 16
COLS = 64
WIDE = COLS + 8
CHUNK = 512
STEP_ROWS = CHUNK // COLS


def dot(a, b):
    return jnp.dot(a, b, preferred_element_type=F32)


def dot_t(a, b):
    return lax.dot_general(a, b, (((1,), (1,)), ((), ())), preferred_element_type=F32)


def xor4(a, b):
    return lax.rem(a + b, 2) + 2 * lax.rem(a // 2 + b // 2, 2)


def slide(ref, start, rows):
    first = lax.div(start, 8)
    off = start - 8 * first
    tiles = ref[pl.ds(first, rows // 8 + 3)]
    for by in (4, 2, 1):
        count = tiles.shape[0] - 1
        place = lax.broadcasted_iota(jnp.int32, (count, 8, C), 1)
        moved = pltpu.roll(tiles, 8 - by, 1)
        bit = jnp.full((count, 8, C), lax.rem(lax.div(off, by), 2), jnp.int32)
        tiles = jnp.where(bit == 1, jnp.where(place < 8 - by, moved[:-1], moved[1:]), tiles[:-1])
    return tiles.reshape(rows, C)


def phase_key(u):
    return 2 * lax.rem(u, 2) + u // 2


def block_kernel(
    shift_ref, rows_hbm, taps, w_in_hbm, w_out_hbm, cot_hbm,
    out_hbm, back_hbm, grads_out, gk_out,
    rowb, rowf, pieces, chain, cotv, w_in, w_out, wide, nhat, rinv, normed, gn, gdp, ghalo_s, ghalo_r,
    strip, outv, gw, gsend, grecv, rs_send, rs_recv, lat_send, lat_recv, ag, gk_mine, gk_lat, gk_all,
    load_sem, fwd_send, fwd_recv, halo_send, halo_recv, gh_send, gh_recv, bwd_send, bwd_recv, out_sem, self_sem,
    core_send, core_recv, rs_ssem, rs_rsem, lat_ssem, lat_rsem, ag_ssem, ag_rsem, full_ssem, full_rsem,
    gkl_ssem, gkl_rsem, gka_ssem, gka_rsem,
):
    me = lax.axis_index("lon")
    lat = lax.axis_index("lat")
    x = me // 16
    z = lax.rem(me // 4, 4)
    cls = lax.rem(me, 4)
    core = lax.rem(me, 2)
    chip = me // 2
    other_lat = (me, 1 - lat)
    other_core = (me + 1 - 2 * core, lat)

    def remote(src, dst, ssem, rsem, device):
        return pltpu.make_async_remote_copy(
            src_ref=src, dst_ref=dst, send_sem=ssem, recv_sem=rsem, device_id=device, device_id_type=MESH
        )

    def peer(s, k):
        m = lax.rem(5 * s, 16)
        return lax.rem(x + m // 4, 4) * 16 + lax.rem(z + lax.rem(m, 4), 4) * 4 + xor4(cls, k)

    barrier = pltpu.get_barrier_semaphore()

    def greet(s, _):
        pl.semaphore_signal(barrier, inc=1, device_id=(lax.rem(me + s, DEVS), lat), device_id_type=MESH)
        return 0

    load_rows = pltpu.make_async_copy(rows_hbm, rowb, load_sem.at[0])
    load_rows.start()
    lax.fori_loop(1, DEVS, greet, 0)
    pl.semaphore_signal(barrier, inc=1, device_id=other_lat, device_id_type=MESH)
    load_w_in = pltpu.make_async_copy(w_in_hbm, w_in, load_sem.at[1])
    load_w_out = pltpu.make_async_copy(w_out_hbm, w_out, load_sem.at[2])
    load_w_in.start()
    load_w_out.start()
    for q in range(CHAINS):
        pltpu.make_async_copy(cot_hbm.at[:, q], cotv.at[q], load_sem.at[3 + q]).start()

    no_row = 17 * lat
    for q in range(CHAINS):
        chain[q, no_row] = jnp.zeros((WIDE, C), BF16)

    def zero_gdp(r, _):
        for b in range(2):
            gdp[b, r] = jnp.zeros((WIDE + 8, C), F32)
        return 0

    lax.fori_loop(0, ROWS + 2, zero_gdp, 0)

    def zero_gw(r, _):
        for g in range(2):
            gw[g, pl.ds(pl.multiple_of(r * 16, 16), 16)] = jnp.zeros((16, FF), F32)
        return 0

    lax.fori_loop(0, 16, zero_gw, 0)

    load_rows.wait()

    def widen(r, _):
        rowf[pl.ds(8 * r, 8)] = rowb[pl.ds(pl.multiple_of(r * 64, 64), 64)].astype(F32).reshape(8, 8, C)
        return 0

    lax.fori_loop(0, NLON // 64, widen, 0)
    rowf[NLON // 8 : NLON // 8 + 12] = rowb[:96].astype(F32).reshape(12, 8, C)
    shift = shift_ref[0]

    def cut(target):
        start = lax.rem(target * COLS + (NLON - 4) + shift, NLON)
        pieces[target] = slide(rowf, start, WIDE).astype(BF16)

    pl.semaphore_wait(barrier, DEVS)

    my_slot = 1 + me // 4
    cut(me)
    own = pltpu.make_async_copy(pieces.at[me], chain.at[cls, my_slot], self_sem.at[0])
    own.start()

    def send_piece(n, _):
        target = peer(lax.rem(n, 16), phase_key(n // 16))
        cut(target)
        remote(pieces.at[target], chain.at[cls, my_slot], fwd_send, fwd_recv.at[cls], (target, lat)).start()
        return 0

    lax.fori_loop(1, DEVS, send_piece, 0)

    edge = ROWS - (ROWS - 1) * lat
    beside = 17 * (1 - lat)

    def halo_copy(q):
        return remote(chain.at[q, edge], chain.at[q, 17 * lat], halo_send.at[q], halo_recv.at[q], other_lat)

    def halo_arrived(q):
        remote(chain.at[q, edge], chain.at[q, beside], halo_send.at[q], halo_recv.at[q], other_lat).wait_recv()

    def arrive(first, q):
        count = ROWS - 1 if first else ROWS
        some = chain.at[q, pl.ds(1, count)]
        remote(some, some, fwd_send, fwd_recv.at[q], other_lat).wait_recv()
        halo_copy(q).start()

    own.wait()
    arrive(True, cls)
    load_w_in.wait()
    load_w_out.wait()
    for q in range(CHAINS):
        pltpu.make_async_copy(cot_hbm.at[:, q], cotv.at[q], load_sem.at[3 + q]).wait()

    def forward(q):
        def to_wide(r, _):
            wide[r] = chain[q, r].astype(F32)
            return 0

        lax.fori_loop(0, ROWS + 2, to_wide, 0)

        def row(t, _):
            depth = None
            for a in range(3):
                for b in range(3):
                    term = taps[3 * a + b : 3 * a + b + 1, :] * wide[t + a, 4 * b : 4 * b + COLS, :]
                    depth = term if depth is None else depth + term
            mean = jnp.mean(depth, axis=-1, keepdims=True)
            centred = depth - mean
            r = lax.rsqrt(jnp.mean(centred * centred, axis=-1, keepdims=True) + EPS)
            n = centred * r
            nhat[t] = n
            rinv[t] = jnp.broadcast_to(r, (COLS, 128))
            normed[t] = n.astype(BF16)
            return 0

        lax.fori_loop(0, ROWS, row, 0)

    def mlp(q):
        def step(h, _):
            at = pl.ds(h * STEP_ROWS, STEP_ROWS)
            nb = normed[at].reshape(CHUNK, C)
            cb = cotv[q, at].reshape(CHUNK, C)
            nbt = nb.T
            cbt = cb.T
            mlp_out = None
            g_norm = None
            for f in range(FF // 256):
                cols = slice(256 * f, 256 * f + 256)
                hid = dot(nb, w_in[:, cols])
                g_act = dot_t(cb, w_out[cols, :])
                h2 = hid * hid
                t = jnp.tanh(hid * (GELU_C + (GELU_C * GELU_A) * h2))
                p = 0.5 + 0.5 * t
                value = hid * p
                slope = p + value * (0.5 - 0.5 * t) * (2.0 * GELU_C + (6.0 * GELU_A * GELU_C) * h2)
                act = value.astype(BF16)
                g_hid = (g_act * slope).astype(BF16)
                out_part = dot(act, w_out[cols, :])
                norm_part = dot_t(g_hid, w_in[:, cols])
                mlp_out = out_part if mlp_out is None else mlp_out + out_part
                g_norm = norm_part if g_norm is None else g_norm + norm_part
                gw[0, :, cols] += dot(nbt, g_hid)
                gw[1, :, cols] += dot(cbt, act)
            gn[at] = g_norm.reshape(STEP_ROWS, COLS, C)
            centre = wide[pl.ds(1 + h * STEP_ROWS, STEP_ROWS), 4 : 4 + COLS, :]
            outv[q, at] = (centre + mlp_out.reshape(STEP_ROWS, COLS, C)).astype(BF16)
            return 0

        lax.fori_loop(0, ROWS // STEP_ROWS, step, 0)
        pltpu.make_async_copy(outv.at[q], out_hbm.at[:, q], out_sem.at[q]).start()

    def norm_back(q, buf, sums):
        def row(t, sums):
            n = nhat[t]
            g = gn[t]
            g_mean = jnp.mean(g, axis=-1, keepdims=True)
            g_proj = jnp.mean(g * n, axis=-1, keepdims=True)
            g_dw = (rinv[t][:, :1] * (g - g_mean - n * g_proj)).astype(BF16)
            wide_g = g_dw.astype(F32)
            gdp[buf, t + 1, 8 : 8 + COLS, :] = wide_g
            new = []
            for a in range(3):
                for b in range(3):
                    prod = wide[t + a, 4 * b : 4 * b + COLS, :] * wide_g
                    new.append(sums[3 * a + b] + jnp.sum(prod.reshape(COLS // 8, 8, C), axis=0))
            return tuple(new)

        sums = lax.fori_loop(0, ROWS, row, sums)
        ghalo_s[q] = gdp[buf, edge, 8 : 8 + COLS, :].astype(BF16)
        return sums

    def ghalo_copy(q):
        return remote(ghalo_s.at[q], ghalo_r.at[q], gh_send.at[q], gh_recv.at[q], other_lat)

    def back_row(q, buf, target):
        t = target // 4
        acc = None
        for a in range(3):
            for b in range(3):
                term = taps[3 * a + b : 3 * a + b + 1, :] * gdp[buf, t + 2 - a, 8 - 4 * b : 8 - 4 * b + WIDE, :]
                acc = term if acc is None else acc + term
        strip[...] = acc
        strip[4 : 4 + COLS, :] = strip[4 : 4 + COLS, :] + cotv[q, t].astype(F32)
        pieces[target] = strip[...].astype(BF16)

    def conv_back(u, q, buf):
        remote(ghalo_s.at[q], ghalo_r.at[q], gh_send.at[q], gh_recv.at[q], other_lat).wait_recv()
        gdp[buf, beside, 8 : 8 + COLS, :] = ghalo_r[q].astype(F32)

        def send(s, _):
            target = peer(s, phase_key(u))
            back_row(q, buf, target)
            remote(pieces.at[target], back_hbm.at[me], bwd_send, bwd_recv, (target, lat)).start()
            return 0

        @pl.when(u == 0)
        def _():
            back_row(q, buf, me)
            pltpu.make_async_copy(pieces.at[me], back_hbm.at[me], self_sem.at[1]).start()

        @pl.when(u > 0)
        def _():
            send(0, 0)

        lax.fori_loop(1, ROWS, send, 0)

    def chain_step(u, sums):
        q = xor4(cls, phase_key(u))
        buf = lax.rem(u, 2)
        halo_arrived(q)
        forward(q)

        @pl.when(u < CHAINS - 1)
        def _():
            arrive(False, xor4(cls, phase_key(u + 1)))

        mlp(q)
        sums = norm_back(q, buf, sums)
        ghalo_copy(q).start()

        @pl.when(u == 1)
        def _():
            remote(pieces.at[pl.ds(1, DEVS - 1)], pieces.at[pl.ds(1, DEVS - 1)], fwd_send, fwd_recv.at[0], other_lat).wait_send()

        @pl.when(u > 0)
        def _():
            conv_back(u - 1, xor4(cls, phase_key(u - 1)), 1 - buf)

        return sums

    sums = lax.fori_loop(0, CHAINS, chain_step, tuple(jnp.zeros((8, C), F32) for _ in range(9)))

    def halve(dst, src):
        def go(r, _):
            dst[r] = src[pl.ds(pl.multiple_of(r * 8, 8), 8), :].astype(BF16)
            return 0

        lax.fori_loop(0, 32, go, 0)

    halve(gsend, gw.at[1 - core])
    core_copy = remote(gsend, grecv, core_send, core_recv, other_core)
    core_copy.start()
    for j in range(9):
        gk_mine[j : j + 1, :] = jnp.sum(sums[j], axis=0, keepdims=True)
    gk_lat_copy = remote(gk_mine, gk_lat, gkl_ssem, gkl_rsem, other_lat)
    gk_lat_copy.start()

    conv_back(CHAINS - 1, xor4(cls, phase_key(CHAINS - 1)), (CHAINS - 1) % 2)

    core_copy.wait()

    def pair(r, _):
        s = gw[core, pl.ds(pl.multiple_of(r * 8, 8), 8), :] + grecv[r].astype(F32)
        rs_send[r] = s.astype(BF16)
        return 0

    lax.fori_loop(0, 32, pair, 0)

    def chip_peer(s):
        m = lax.rem(11 * s, 32)
        yh = lax.rem(chip + m, 2)
        xz = lax.rem(chip // 2 + m // 2 , 16)
        return xz * 2 + yh

    def rs_go(s, _):
        p = chip_peer(s)
        remote(rs_send.at[p], rs_recv.at[chip], rs_ssem, rs_rsem, (2 * p + core, lat)).start()
        return 0

    lax.fori_loop(1, 32, rs_go, 0)

    gk_lat_copy.wait()
    gk_all[me] = gk_mine[...] + gk_lat[...]

    def gk_go(s, _):
        p = lax.rem(me + s, DEVS)
        remote(gk_all.at[me], gk_all.at[me], gka_ssem, gka_rsem, (p, lat)).start()
        return 0

    lax.fori_loop(1, DEVS, gk_go, 0)

    rs_all = rs_send.at[pl.ds(1, 31)]
    remote(rs_all, rs_recv.at[pl.ds(1, 31)], rs_ssem, rs_rsem, other_lat).wait()
    rs_recv[chip] = rs_send[chip]

    def rs_sum(r, s):
        return s + rs_recv[r].astype(F32)

    lat_send[...] = lax.fori_loop(0, 32, rs_sum, jnp.zeros((8, FF), F32))
    lat_copy = remote(lat_send, lat_recv, lat_ssem, lat_rsem, other_lat)
    lat_copy.start()
    lat_copy.wait()
    ag[core, chip] = (lat_send[...] + lat_recv[...]).astype(BF16)

    def ag_go(s, _):
        p = chip_peer(s)
        remote(ag.at[core, chip], ag.at[core, chip], ag_ssem, ag_rsem, (2 * p + core, lat)).start()
        return 0

    lax.fori_loop(1, 32, ag_go, 0)
    ag_all = ag.at[core, pl.ds(1, 31)]
    remote(ag_all, ag_all, ag_ssem, ag_rsem, other_lat).wait()
    full = remote(ag.at[core], ag.at[core], full_ssem, full_rsem, other_core)
    full.start()
    gk_rest = gk_all.at[pl.ds(1, DEVS - 1)]
    remote(gk_rest, gk_rest, gka_ssem, gka_rsem, other_lat).wait()

    def gk_sum(r, s):
        return s + gk_all[r]

    gk_out[...] = lax.fori_loop(0, DEVS, gk_sum, jnp.zeros((16, C), F32))
    full.wait()
    save = pltpu.make_async_copy(ag, grads_out, self_sem.at[2])
    save.start()

    pltpu.make_async_copy(pieces.at[me], back_hbm.at[me], self_sem.at[1]).wait()
    for q in range(CHAINS):
        halo_copy(q).wait_send()
        ghalo_copy(q).wait_send()
        pltpu.make_async_copy(outv.at[q], out_hbm.at[:, q], out_sem.at[q]).wait()
    back_rest = back_hbm.at[pl.ds(1, DEVS - 1)]
    remote(pieces.at[pl.ds(1, DEVS - 1)], back_rest, bwd_send, bwd_recv, other_lat).wait()
    save.wait()


def finish_kernel(shift_ref, scale, back, out_tmp, grads, gk, rows_ref, out_ref, gwi_ref, gwo_ref, gk_ref, full, sem):
    copy = pltpu.make_async_copy(out_tmp, out_ref, sem)
    copy.start()
    span = 256
    full[0] = jnp.zeros((8, C), F32)

    def gather(j, _):
        piece = back[j].astype(F32).reshape(9, 8, C)
        full[8 * j] += piece[0]
        full[pl.ds(8 * j + 1, 8)] = piece[1:]
        return 0

    lax.fori_loop(0, DEVS, gather, 0)
    seam = full[0] + full[NLON // 8]
    full[0] = seam
    full[NLON // 8] = seam
    full[NLON // 8 + 1 : NLON // 8 + 4 + span // 8] = full[1 : 4 + span // 8]
    shift = shift_ref[0]

    def emit(r, _):
        start = lax.rem(r * span + NLON - shift, NLON) + 4
        rows_ref[pl.ds(pl.multiple_of(r * span, span), span), :] = slide(full, start, span).astype(BF16)
        return 0

    lax.fori_loop(0, NLON // span, emit, 0)
    gwi_ref[...] = scale * grads[0].reshape(C, FF).astype(F32)
    gwo_ref[...] = (scale * grads[1].reshape(C, FF).astype(F32)).T
    gk_ref[...] = scale * gk[:9]
    copy.wait()


def shards(rows_in, row_shift, kernel, w_in, w_out, cotangent):
    hbm = pl.BlockSpec(memory_space=pltpu.HBM)
    vmem = pl.BlockSpec(memory_space=pltpu.VMEM)
    smem = pl.BlockSpec(memory_space=pltpu.SMEM)
    dma = pltpu.SemaphoreType.DMA
    v = pltpu.VMEM
    out_tmp, back, grads, gk = pl.pallas_call(
        block_kernel,
        out_shape=(
            jax.ShapeDtypeStruct((ROWS, CHAINS, COLS, C), BF16),
            jax.ShapeDtypeStruct((DEVS, WIDE, C), BF16),
            jax.ShapeDtypeStruct((2, 32, 8, FF), BF16),
            jax.ShapeDtypeStruct((16, C), F32),
        ),
        in_specs=[smem, hbm, vmem, hbm, hbm, hbm],
        out_specs=(hbm, hbm, hbm, vmem),
        scratch_shapes=[
            v((NLON, C), BF16), v((NLON // 8 + 12, 8, C), F32), v((DEVS, WIDE, C), BF16),
            v((CHAINS, ROWS + 2, WIDE, C), BF16), v((CHAINS, ROWS, COLS, C), BF16),
            v((C, FF), BF16), v((FF, C), BF16), v((ROWS + 2, WIDE, C), F32),
            v((ROWS, COLS, C), F32), v((ROWS, COLS, 128), F32), v((ROWS, COLS, C), BF16),
            v((ROWS, COLS, C), F32), v((2, ROWS + 2, WIDE + 8, C), F32),
            v((CHAINS, COLS, C), BF16), v((CHAINS, COLS, C), BF16), v((WIDE, C), F32),
            v((CHAINS, ROWS, COLS, C), BF16), v((2, C, FF), F32),
            v((32, 8, FF), BF16), v((32, 8, FF), BF16), v((32, 8, FF), BF16), v((32, 8, FF), BF16),
            v((8, FF), F32), v((8, FF), F32), v((2, 32, 8, FF), BF16),
            v((16, C), F32), v((16, C), F32), v((DEVS, 16, C), F32),
            dma((7,)), dma, dma((4,)), dma((4,)), dma((4,)), dma((4,)), dma((4,)), dma, dma, dma((4,)), dma((3,)),
            dma, dma, dma, dma, dma, dma, dma, dma, dma, dma, dma, dma, dma, dma,
        ],
        compiler_params=pltpu.CompilerParams(
            collective_id=0, has_side_effects=True, vmem_limit_bytes=58 << 20
        ),
        name="block",
    )(row_shift, rows_in[0], kernel, w_in, w_out, cotangent.reshape(ROWS, CHAINS, COLS, C))
    scale = 1.0 / math.sqrt(2 * DEVS * NLON)
    rows, out, grad_in, grad_out, grad_kernel = pl.pallas_call(
        lambda shift_ref, *refs: finish_kernel(shift_ref, scale, *refs),
        out_shape=(
            jax.ShapeDtypeStruct((NLON, C), BF16),
            jax.ShapeDtypeStruct((ROWS, CHAINS, COLS, C), BF16),
            jax.ShapeDtypeStruct((C, FF), F32),
            jax.ShapeDtypeStruct((FF, C), F32),
            jax.ShapeDtypeStruct((9, C), F32),
        ),
        in_specs=[smem, vmem, hbm, vmem, vmem],
        out_specs=(vmem, hbm, vmem, vmem, vmem),
        scratch_shapes=[v((NLON // 8 + 36, 8, C), F32), dma],
        compiler_params=pltpu.CompilerParams(vmem_limit_bytes=40 << 20),
        name="finish",
    )(row_shift, back, out_tmp, grads, gk)
    return (
        out.reshape(ROWS * CHAINS, COLS, C),
        rows[None],
        grad_kernel,
        grad_in,
        grad_out,
    )


def solution(mesh):
    in_specs = (
        P(("lat", "lon"), None, None),
        P(("lat", "lon")),
        P(),
        P(),
        P(),
        P("lat", "lon", None),
    )
    out_specs = (P("lat", "lon", None), P(("lat", "lon"), None, None), P(), P(), P())
    return jax.shard_map(shards, mesh=mesh, in_specs=in_specs, out_specs=out_specs, check_vma=False)
```

```python
import functools
import math

import jax
import jax.numpy as jnp
from jax import lax
from jax.experimental import pallas as pl
from jax.experimental.pallas import tpu as pltpu
from jax.sharding import PartitionSpec as P

MESH = pl.DeviceIdType.MESH
GELU_C = math.sqrt(2.0 / math.pi)
GELU_A = 0.044715
EPS = 1e-06
F32 = jnp.float32
BF16 = jnp.bfloat16

NLON = 4096
C = 256
FF = 1024
DEVS = 64
CHAINS = 4
ROWS = 16
COLS = 64
WIDE = COLS + 8
CHUNK = 512
STEP_ROWS = CHUNK // COLS


def dot(a, b):
    return jnp.dot(a, b, preferred_element_type=F32)


def dot_t(a, b):
    return lax.dot_general(a, b, (((1,), (1,)), ((), ())), preferred_element_type=F32)


def xor4(a, b):
    return lax.rem(a + b, 2) + 2 * lax.rem(a // 2 + b // 2, 2)


def slide(ref, start, rows):
    first = lax.div(start, 8)
    off = start - 8 * first
    tiles = ref[pl.ds(first, rows // 8 + 3)].astype(F32)
    for by in (4, 2, 1):
        count = tiles.shape[0] - 1
        place = lax.broadcasted_iota(jnp.int32, (count, 8, C), 1)
        moved = pltpu.roll(tiles, 8 - by, 1)
        bit = jnp.full((count, 8, C), lax.rem(lax.div(off, by), 2), jnp.int32)
        tiles = jnp.where(bit == 1, jnp.where(place < 8 - by, moved[:-1], moved[1:]), tiles[:-1])
    return tiles.reshape(rows, C)


def phase_key(u):
    return 2 * lax.rem(u + u // 2, 2) + u // 2


def block_kernel(
    shift_ref, rows_hbm, taps, w_in_hbm, w_out_hbm, cot_hbm,
    out_hbm, back_hbm, grads_out, gk_out,
    rowb, pieces, back_pieces, chain, cotv, w_in, w_out, wide, nhat, rinv, normed, gn, gdp, ghalo_s, ghalo_r,
    strip, outv, gw, gsend, grecv, rs_send, rs_recv, lat_send, lat_recv, ag, gk_mine, gk_lat, gk_all,
    load_sem, fwd_send, fwd_recv, halo_send, halo_recv, gh_send, gh_recv, bwd_send, bwd_recv, out_sem, self_sem,
    core_send, core_recv, rs_ssem, rs_rsem, lat_ssem, lat_rsem, ag_ssem, ag_rsem, full_ssem, full_rsem,
    gkl_ssem, gkl_rsem, gka_ssem, gka_rsem,
):
    me = lax.axis_index("lon")
    lat = lax.axis_index("lat")
    x = me // 16
    z = lax.rem(me // 4, 4)
    cls = lax.rem(me, 4)
    core = lax.rem(me, 2)
    chip = me // 2
    other_lat = (me, 1 - lat)
    other_core = (me + 1 - 2 * core, lat)

    def remote(src, dst, ssem, rsem, device):
        return pltpu.make_async_remote_copy(
            src_ref=src, dst_ref=dst, send_sem=ssem, recv_sem=rsem, device_id=device, device_id_type=MESH
        )

    def place(s):
        m = lax.rem(5 * s, 16)
        return lax.rem(x + m // 4, 4), lax.rem(z + lax.rem(m, 4), 4)

    def chain_at(x, z, cls, u):
        return xor4(xor4(cls, phase_key(u)), 2 * lax.rem(x + z, 2))

    def chain_of(u):
        return chain_at(x, z, cls, u)

    barrier = pltpu.get_barrier_semaphore()

    def greet(s, _):
        pl.semaphore_signal(barrier, inc=1, device_id=(lax.rem(me + s, DEVS), lat), device_id_type=MESH)
        return 0

    load_rows = pltpu.make_async_copy(rows_hbm, rowb.at[pl.ds(0, NLON // 8)], load_sem.at[0])
    load_wrap = pltpu.make_async_copy(rows_hbm.at[pl.ds(0, 12)], rowb.at[pl.ds(NLON // 8, 12)], load_sem.at[7])
    load_rows.start()
    load_wrap.start()
    lax.fori_loop(1, DEVS, greet, 0)
    pl.semaphore_signal(barrier, inc=1, device_id=other_lat, device_id_type=MESH)
    load_rows.wait()
    load_wrap.wait()
    shift = shift_ref[0]

    def cut(target):
        start = lax.rem(target * COLS + (NLON - 4) + shift, NLON)
        pieces[target] = slide(rowb, start, WIDE).astype(BF16)

    pl.semaphore_wait(barrier, DEVS)

    my_slot = 1 + me // 4

    def send_phase(u):
        def send(s, _):
            tx, tz = place(s)
            target = tx * 16 + tz * 4 + chain_at(tx, tz, cls, u)
            cut(target)

            @pl.when(target != me)
            def _():
                remote(pieces.at[target], chain.at[cls, my_slot], fwd_send, fwd_recv.at[cls], (target, lat)).start()

            @pl.when(target == me)
            def _():
                pltpu.make_async_copy(pieces.at[me], chain.at[cls, my_slot], self_sem.at[0]).start()

            return 0

        lax.fori_loop(0, ROWS, send, 0)

    send_phase(0)

    load_w_in = pltpu.make_async_copy(w_in_hbm, w_in, load_sem.at[1])
    load_w_out = pltpu.make_async_copy(w_out_hbm, w_out, load_sem.at[2])
    load_w_in.start()
    load_w_out.start()
    for q in range(CHAINS):
        pltpu.make_async_copy(cot_hbm.at[:, q], cotv.at[q], load_sem.at[3 + q]).start()

    no_row = 17 * lat
    for q in range(CHAINS):
        chain[q, no_row] = jnp.zeros((WIDE, C), BF16)

    def zero_gdp(r, _):
        for b in range(2):
            gdp[b, r] = jnp.zeros((WIDE + 8, C), F32)
        return 0

    lax.fori_loop(0, ROWS + 2, zero_gdp, 0)

    def zero_gw(r, _):
        for g in range(2):
            gw[g, pl.ds(pl.multiple_of(r * 16, 16), 16)] = jnp.zeros((16, FF), F32)
        return 0

    lax.fori_loop(0, 16, zero_gw, 0)

    edge = ROWS - (ROWS - 1) * lat
    beside = 17 * (1 - lat)

    def halo_copy(q):
        return remote(chain.at[q, edge], chain.at[q, 17 * lat], halo_send.at[q], halo_recv.at[q], other_lat)

    def halo_arrived(q):
        remote(chain.at[q, edge], chain.at[q, beside], halo_send.at[q], halo_recv.at[q], other_lat).wait_recv()

    def arrive(u):
        q = chain_of(u)

        @pl.when(q == cls)
        def _():
            some = chain.at[q, pl.ds(1, ROWS - 1)]
            remote(some, some, fwd_send, fwd_recv.at[q], other_lat).wait_recv()
            pltpu.make_async_copy(pieces.at[me], chain.at[cls, my_slot], self_sem.at[0]).wait()

        @pl.when(q != cls)
        def _():
            some = chain.at[q, pl.ds(1, ROWS)]
            remote(some, some, fwd_send, fwd_recv.at[q], other_lat).wait_recv()

        halo_copy(q).start()

    arrive(0)
    send_phase(1)
    load_w_in.wait()
    load_w_out.wait()
    for q in range(CHAINS):
        pltpu.make_async_copy(cot_hbm.at[:, q], cotv.at[q], load_sem.at[3 + q]).wait()

    def forward(q):
        def to_wide(r, _):
            wide[r] = chain[q, r].astype(F32)
            return 0

        lax.fori_loop(0, ROWS + 2, to_wide, 0)

        def row(t, _):
            depth = None
            for a in range(3):
                for b in range(3):
                    term = taps[3 * a + b : 3 * a + b + 1, :] * wide[t + a, 4 * b : 4 * b + COLS, :]
                    depth = term if depth is None else depth + term
            mean = jnp.mean(depth, axis=-1, keepdims=True)
            centred = depth - mean
            r = lax.rsqrt(jnp.mean(centred * centred, axis=-1, keepdims=True) + EPS)
            n = centred * r
            nhat[t] = n
            rinv[t] = jnp.broadcast_to(r, (COLS, 128))
            normed[t] = n.astype(BF16)
            return 0

        lax.fori_loop(0, ROWS, row, 0)

    def mlp(q):
        def step(h, _):
            at = pl.ds(h * STEP_ROWS, STEP_ROWS)
            nb = normed[at].reshape(CHUNK, C)
            cb = cotv[q, at].reshape(CHUNK, C)
            nbt = nb.T
            cbt = cb.T
            mlp_out = None
            g_norm = None
            for f in range(FF // 256):
                cols = slice(256 * f, 256 * f + 256)
                hid = dot(nb, w_in[:, cols])
                g_act = dot_t(cb, w_out[cols, :])
                h2 = hid * hid
                t = jnp.tanh(hid * (GELU_C + (GELU_C * GELU_A) * h2))
                p = 0.5 + 0.5 * t
                value = hid * p
                slope = p + value * (0.5 - 0.5 * t) * (2.0 * GELU_C + (6.0 * GELU_A * GELU_C) * h2)
                act = value.astype(BF16)
                g_hid = (g_act * slope).astype(BF16)
                out_part = dot(act, w_out[cols, :])
                norm_part = dot_t(g_hid, w_in[:, cols])
                mlp_out = out_part if mlp_out is None else mlp_out + out_part
                g_norm = norm_part if g_norm is None else g_norm + norm_part
                gw[0, :, cols] += dot(nbt, g_hid)
                gw[1, :, cols] += dot(cbt, act)
            gn[at] = g_norm.reshape(STEP_ROWS, COLS, C)
            centre = wide[pl.ds(1 + h * STEP_ROWS, STEP_ROWS), 4 : 4 + COLS, :]
            outv[q, at] = (centre + mlp_out.reshape(STEP_ROWS, COLS, C)).astype(BF16)
            return 0

        lax.fori_loop(0, ROWS // STEP_ROWS, step, 0)
        pltpu.make_async_copy(outv.at[q], out_hbm.at[:, q], out_sem.at[q]).start()

    def norm_back(q, buf, sums):
        def row(t, sums):
            n = nhat[t]
            g = gn[t]
            g_mean = jnp.mean(g, axis=-1, keepdims=True)
            g_proj = jnp.mean(g * n, axis=-1, keepdims=True)
            g_dw = (rinv[t][:, :1] * (g - g_mean - n * g_proj)).astype(BF16)
            wide_g = g_dw.astype(F32)
            gdp[buf, t + 1, 8 : 8 + COLS, :] = wide_g
            new = []
            for a in range(3):
                for b in range(3):
                    prod = wide[t + a, 4 * b : 4 * b + COLS, :] * wide_g
                    new.append(sums[3 * a + b] + jnp.sum(prod.reshape(COLS // 8, 8, C), axis=0))
            return tuple(new)

        sums = lax.fori_loop(0, ROWS, row, sums)
        ghalo_s[q] = gdp[buf, edge, 8 : 8 + COLS, :].astype(BF16)
        return sums

    def ghalo_copy(q):
        return remote(ghalo_s.at[q], ghalo_r.at[q], gh_send.at[q], gh_recv.at[q], other_lat)

    def back_row(q, buf, target):
        t = target // 4
        acc = None
        for a in range(3):
            for b in range(3):
                term = taps[3 * a + b : 3 * a + b + 1, :] * gdp[buf, t + 2 - a, 8 - 4 * b : 8 - 4 * b + WIDE, :]
                acc = term if acc is None else acc + term
        strip[...] = acc
        strip[4 : 4 + COLS, :] = strip[4 : 4 + COLS, :] + cotv[q, t].astype(F32)
        back_pieces[target] = strip[...].astype(BF16)

    def conv_back(q, buf):
        remote(ghalo_s.at[q], ghalo_r.at[q], gh_send.at[q], gh_recv.at[q], other_lat).wait_recv()
        gdp[buf, beside, 8 : 8 + COLS, :] = ghalo_r[q].astype(F32)

        def send(s, _):
            tx, tz = place(s)
            target = tx * 16 + tz * 4 + q
            back_row(q, buf, target)

            @pl.when(target != me)
            def _():
                remote(back_pieces.at[target], back_hbm.at[me], bwd_send, bwd_recv, (target, lat)).start()

            @pl.when(target == me)
            def _():
                pltpu.make_async_copy(back_pieces.at[me], back_hbm.at[me], self_sem.at[1]).start()

            return 0

        lax.fori_loop(0, ROWS, send, 0)

    def chain_step(u, sums):
        q = chain_of(u)
        buf = lax.rem(u, 2)
        halo_arrived(q)
        forward(q)

        @pl.when(u > 0)
        def _():
            conv_back(chain_of(u - 1), 1 - buf)

        mlp(q)
        arrive(u + 1)
        sums = norm_back(q, buf, sums)
        ghalo_copy(q).start()

        @pl.when(u < CHAINS - 2)
        def _():
            send_phase(u + 2)

        return sums

    last = CHAINS - 1
    sums = lax.fori_loop(0, last, chain_step, tuple(jnp.zeros((8, C), F32) for _ in range(9)))
    q = chain_of(last)
    halo_arrived(q)
    forward(q)
    conv_back(chain_of(last - 1), (last - 1) % 2)
    mlp(q)

    def halve(r, _):
        gsend[r] = gw[1 - core, pl.ds(pl.multiple_of(r * 8, 8), 8), :].astype(BF16)
        return 0

    lax.fori_loop(0, 32, halve, 0)
    core_copy = remote(gsend, grecv, core_send, core_recv, other_core)
    core_copy.start()

    sums = norm_back(q, last % 2, sums)
    ghalo_copy(q).start()
    for j in range(9):
        gk_mine[j : j + 1, :] = jnp.sum(sums[j], axis=0, keepdims=True)
    gk_lat_copy = remote(gk_mine, gk_lat, gkl_ssem, gkl_rsem, other_lat)
    gk_lat_copy.start()

    core_copy.wait()

    def pair(r, _):
        s = gw[core, pl.ds(pl.multiple_of(r * 8, 8), 8), :] + grecv[r].astype(F32)
        rs_send[r] = s.astype(BF16)
        return 0

    lax.fori_loop(0, 32, pair, 0)

    def chip_peer(s):
        m = lax.rem(11 * s, 32)
        yh = lax.rem(chip + m, 2)
        xz = lax.rem(chip // 2 + m // 2, 16)
        return xz * 2 + yh

    def rs_go(s, _):
        p = chip_peer(s)
        remote(rs_send.at[p], rs_recv.at[chip], rs_ssem, rs_rsem, (2 * p + core, lat)).start()
        return 0

    lax.fori_loop(1, 32, rs_go, 0)

    places = (x, z, cls)

    def gk_device(stage, other):
        at = [other if stage == n else places[n] for n in range(3)]
        return (at[0] * 16 + at[1] * 4 + at[2], lat)

    def gk_start(stage, value):
        mine = places[stage]
        gk_all[stage, mine] = value
        for n in range(1, 4):
            slot = gk_all.at[stage, mine]
            remote(slot, slot, gka_ssem.at[stage], gka_rsem.at[stage], gk_device(stage, lax.rem(mine + n, 4))).start()

    def gk_end(stage):
        some = gk_all.at[stage, pl.ds(0, 3)]
        remote(some, some, gka_ssem.at[stage], gka_rsem.at[stage], other_lat).wait()
        return (gk_all[stage, 0] + gk_all[stage, 1]) + (gk_all[stage, 2] + gk_all[stage, 3])

    conv_back(q, last % 2)
    gk_lat_copy.wait()
    gk_start(0, gk_mine[...] + gk_lat[...])

    rs_all = rs_send.at[pl.ds(1, 31)]
    remote(rs_all, rs_recv.at[pl.ds(1, 31)], rs_ssem, rs_rsem, other_lat).wait()
    rs_recv[chip] = rs_send[chip]

    def rs_sum(r, s):
        return s + rs_recv[r].astype(F32)

    lat_send[...] = lax.fori_loop(0, 32, rs_sum, jnp.zeros((8, FF), F32))
    lat_copy = remote(lat_send, lat_recv, lat_ssem, lat_rsem, other_lat)
    lat_copy.start()
    gk_start(1, gk_end(0))
    lat_copy.wait()
    ag[core, chip] = (lat_send[...] + lat_recv[...]).astype(BF16)

    def ag_go(s, _):
        p = chip_peer(s)
        remote(ag.at[core, chip], ag.at[core, chip], ag_ssem, ag_rsem, (2 * p + core, lat)).start()
        return 0

    lax.fori_loop(1, 32, ag_go, 0)
    gk_start(2, gk_end(1))
    ag_all = ag.at[core, pl.ds(1, 31)]
    remote(ag_all, ag_all, ag_ssem, ag_rsem, other_lat).wait()
    full = remote(ag.at[core], ag.at[core], full_ssem, full_rsem, other_core)
    full.start()
    save_mine = pltpu.make_async_copy(ag.at[core], grads_out.at[core], self_sem.at[2])
    save_mine.start()
    gk_out[...] = gk_end(2)
    full.wait()
    save_other = pltpu.make_async_copy(ag.at[1 - core], grads_out.at[1 - core], self_sem.at[3])
    save_other.start()

    pltpu.make_async_copy(back_pieces.at[me], back_hbm.at[me], self_sem.at[1]).wait()
    for q in range(CHAINS):
        halo_copy(q).wait_send()
        ghalo_copy(q).wait_send()
        pltpu.make_async_copy(outv.at[q], out_hbm.at[:, q], out_sem.at[q]).wait()
    fwd_rest = pieces.at[pl.ds(1, DEVS - 1)]
    remote(fwd_rest, fwd_rest, fwd_send, fwd_recv.at[0], other_lat).wait_send()
    back_rest = back_hbm.at[pl.ds(1, DEVS - 1)]
    remote(back_pieces.at[pl.ds(1, DEVS - 1)], back_rest, bwd_send, bwd_recv, other_lat).wait()
    save_mine.wait()
    save_other.wait()


def finish_kernel(
    shift_ref, scale, back, out_tmp, grads, gk, rows_ref, out_ref, gwi_ref, gwo_ref, gk_ref,
    backv, gradv, gkv, rowsv, outv, gwiv, gwov, full, in_sem, out_sem, sem,
):
    groups = 8
    each = DEVS // groups
    span = 256

    def load(g):
        at = pl.ds(g * each, each)
        return pltpu.make_async_copy(back.at[at], backv.at[at], in_sem.at[g])

    for g in range(groups):
        load(g).start()
    load_grads = pltpu.make_async_copy(grads, gradv, sem.at[0])
    load_grads.start()
    load_gk = pltpu.make_async_copy(gk, gkv, sem.at[1])
    load_gk.start()
    take_out = pltpu.make_async_copy(out_tmp, outv, sem.at[2])
    take_out.start()
    full[0] = jnp.zeros((8, C), F32)
    for g in range(groups):
        load(g).wait()

        def gather(n, _):
            j = g * each + n
            piece = backv[j].astype(F32).reshape(9, 8, C)
            full[8 * j] += piece[0]
            full[pl.ds(8 * j + 1, 8)] = piece[1:]
            return 0

        lax.fori_loop(0, each, gather, 0)
    take_out.wait()
    give_out = pltpu.make_async_copy(outv, out_ref, sem.at[2])
    give_out.start()
    seam = full[0] + full[NLON // 8]
    full[0] = seam
    full[NLON // 8] = seam
    full[NLON // 8 + 1 : NLON // 8 + 2 + span // 8] = full[1 : 2 + span // 8]
    shift = shift_ref[0]

    def emit_copy(r):
        at = pl.ds(pl.multiple_of(r * span, span), span)
        return pltpu.make_async_copy(rowsv.at[at], rows_ref.at[at], out_sem)

    def emit(r, _):
        start = lax.rem(r * span + NLON - shift, NLON) + 4
        first = lax.div(start, 8)
        off = start - 8 * first
        tiles = full[pl.ds(first, span // 8 + 1)]
        moved = pltpu.roll(tiles, lax.rem(8 - off, 8), 1)
        stays = lax.broadcasted_iota(jnp.int32, (span // 8, 8, C), 1) < 8 - off
        rows = jnp.where(stays, moved[:-1], moved[1:]).reshape(span, C)
        rowsv[pl.ds(pl.multiple_of(r * span, span), span), :] = rows.astype(BF16)
        emit_copy(r).start()
        return 0

    lax.fori_loop(0, NLON // span, emit, 0)
    load_grads.wait()
    gwiv[...] = scale * gradv[0].reshape(C, FF).astype(F32)
    store_i = pltpu.make_async_copy(gwiv, gwi_ref, sem.at[3])
    store_i.start()
    gwov[...] = (scale * gradv[1].reshape(C, FF).astype(F32)).T
    store_o = pltpu.make_async_copy(gwov, gwo_ref, sem.at[4])
    store_o.start()
    load_gk.wait()
    gk_ref[...] = scale * gkv[:9]
    pltpu.make_async_copy(rowsv, rows_ref, out_sem).wait()
    store_i.wait()
    store_o.wait()
    give_out.wait()


def shards(rows_in, row_shift, kernel, w_in, w_out, cotangent):
    hbm = pl.BlockSpec(memory_space=pltpu.HBM)
    vmem = pl.BlockSpec(memory_space=pltpu.VMEM)
    smem = pl.BlockSpec(memory_space=pltpu.SMEM)
    dma = pltpu.SemaphoreType.DMA
    v = pltpu.VMEM
    out_tmp, back, grads, gk = pl.pallas_call(
        block_kernel,
        out_shape=(
            jax.ShapeDtypeStruct((ROWS, CHAINS, COLS, C), BF16),
            jax.ShapeDtypeStruct((DEVS, WIDE, C), BF16),
            jax.ShapeDtypeStruct((2, 32, 8, FF), BF16),
            jax.ShapeDtypeStruct((16, C), F32),
        ),
        in_specs=[smem, hbm, vmem, hbm, hbm, hbm],
        out_specs=(hbm, hbm, hbm, vmem),
        scratch_shapes=[
            v((NLON // 8 + 12, 8, C), BF16), v((DEVS, WIDE, C), BF16), v((DEVS, WIDE, C), BF16),
            v((CHAINS, ROWS + 2, WIDE, C), BF16), v((CHAINS, ROWS, COLS, C), BF16),
            v((C, FF), BF16), v((FF, C), BF16), v((ROWS + 2, WIDE, C), F32),
            v((ROWS, COLS, C), F32), v((ROWS, COLS, 128), F32), v((ROWS, COLS, C), BF16),
            v((ROWS, COLS, C), F32), v((2, ROWS + 2, WIDE + 8, C), F32),
            v((CHAINS, COLS, C), BF16), v((CHAINS, COLS, C), BF16), v((WIDE, C), F32),
            v((CHAINS, ROWS, COLS, C), BF16), v((2, C, FF), F32),
            v((32, 8, FF), BF16), v((32, 8, FF), BF16), v((32, 8, FF), BF16), v((32, 8, FF), BF16),
            v((8, FF), F32), v((8, FF), F32), v((2, 32, 8, FF), BF16),
            v((16, C), F32), v((16, C), F32), v((3, 4, 16, C), F32),
            dma((8,)), dma, dma((4,)), dma((4,)), dma((4,)), dma((4,)), dma((4,)), dma, dma, dma((4,)), dma((4,)),
            dma, dma, dma, dma, dma, dma, dma, dma, dma, dma, dma, dma, dma((3,)), dma((3,)),
        ],
        compiler_params=pltpu.CompilerParams(
            collective_id=0, has_side_effects=True, vmem_limit_bytes=58 << 20
        ),
        name="block",
    )(row_shift, rows_in.reshape(NLON // 8, 8, C), kernel, w_in, w_out, cotangent.reshape(ROWS, CHAINS, COLS, C))
    scale = 1.0 / math.sqrt(2 * DEVS * NLON)
    rows, out, grad_in, grad_out, grad_kernel = pl.pallas_call(
        lambda shift_ref, *refs: finish_kernel(shift_ref, scale, *refs),
        out_shape=(
            jax.ShapeDtypeStruct((NLON, C), BF16),
            jax.ShapeDtypeStruct((ROWS, CHAINS, COLS, C), BF16),
            jax.ShapeDtypeStruct((C, FF), F32),
            jax.ShapeDtypeStruct((FF, C), F32),
            jax.ShapeDtypeStruct((9, C), F32),
        ),
        in_specs=[smem, hbm, hbm, hbm, hbm],
        out_specs=(hbm, hbm, hbm, hbm, vmem),
        scratch_shapes=[
            v((DEVS, WIDE, C), BF16), v((2, 32, 8, FF), BF16), v((16, C), F32), v((NLON, C), BF16),
            v((ROWS, CHAINS, COLS, C), BF16), v((C, FF), F32), v((FF, C), F32), v((NLON // 8 + 34, 8, C), F32), dma((8,)), dma, dma((5,)),
        ],
        compiler_params=pltpu.CompilerParams(vmem_limit_bytes=58 << 20),
        name="finish",
    )(row_shift, back, out_tmp, grads, gk)
    return (
        out.reshape(ROWS * CHAINS, COLS, C),
        rows[None],
        grad_kernel,
        grad_in,
        grad_out,
    )


def solution(mesh):
    in_specs = (
        P(("lat", "lon"), None, None),
        P(("lat", "lon")),
        P(),
        P(),
        P(),
        P("lat", "lon", None),
    )
    out_specs = (P("lat", "lon", None), P(("lat", "lon"), None, None), P(), P(), P())
    return jax.shard_map(shards, mesh=mesh, in_specs=in_specs, out_specs=out_specs, check_vma=False)
```

```python
import functools
import math

import jax
import jax.numpy as jnp
from jax import lax
from jax.experimental import pallas as pl
from jax.experimental.pallas import tpu as pltpu
from jax.sharding import PartitionSpec as P

MESH = pl.DeviceIdType.MESH
GELU_C = math.sqrt(2.0 / math.pi)
GELU_A = 0.044715
EPS = 1e-06
F32 = jnp.float32
BF16 = jnp.bfloat16

NLON = 4096
C = 256
FF = 1024
DEVS = 64
CHAINS = 4
ROWS = 16
COLS = 64
WIDE = COLS + 8
CHUNK = 512
STEP_ROWS = CHUNK // COLS


def dot(a, b):
    return jnp.dot(a, b, preferred_element_type=F32)


def dot_t(a, b):
    return lax.dot_general(a, b, (((1,), (1,)), ((), ())), preferred_element_type=F32)


def xor4(a, b):
    return lax.rem(a + b, 2) + 2 * lax.rem(a // 2 + b // 2, 2)


def slide(ref, start, rows):
    first = lax.div(start, 8)
    off = start - 8 * first
    tiles = ref[pl.ds(first, rows // 8 + 3)].astype(F32)
    for by in (4, 2, 1):
        count = tiles.shape[0] - 1
        place = lax.broadcasted_iota(jnp.int32, (count, 8, C), 1)
        moved = pltpu.roll(tiles, 8 - by, 1)
        bit = jnp.full((count, 8, C), lax.rem(lax.div(off, by), 2), jnp.int32)
        tiles = jnp.where(bit == 1, jnp.where(place < 8 - by, moved[:-1], moved[1:]), tiles[:-1])
    return tiles.reshape(rows, C)


def phase_key(u):
    return 2 * lax.rem(u + u // 2, 2) + u // 2


def block_kernel(
    shift_ref, rows_hbm, taps, w_in_hbm, w_out_hbm, cot_hbm,
    out_hbm, back_hbm, grads_out, gk_out,
    rowb, pieces, back_pieces, chain, cotv, w_in, w_out, wide, nhat, rinv, normed, gn, gdp, ghalo_s, ghalo_r,
    strip, outv, gw, gsend, grecv, rs_send, rs_recv, lat_send, lat_recv, ag, gk_mine, gk_lat, gk_all,
    load_sem, fwd_send, fwd_recv, halo_send, halo_recv, gh_send, gh_recv, bwd_send, bwd_recv, out_sem, self_sem,
    core_send, core_recv, rs_ssem, rs_rsem, lat_ssem, lat_rsem, ag_ssem, ag_rsem, full_ssem, full_rsem,
    gkl_ssem, gkl_rsem, gka_ssem, gka_rsem,
):
    me = lax.axis_index("lon")
    lat = lax.axis_index("lat")
    x = me // 16
    z = lax.rem(me // 4, 4)
    cls = lax.rem(me, 4)
    core = lax.rem(me, 2)
    chip = me // 2
    other_lat = (me, 1 - lat)
    other_core = (me + 1 - 2 * core, lat)

    def remote(src, dst, ssem, rsem, device):
        return pltpu.make_async_remote_copy(
            src_ref=src, dst_ref=dst, send_sem=ssem, recv_sem=rsem, device_id=device, device_id_type=MESH
        )

    def place(s):
        m = lax.rem(5 * s, 16)
        return lax.rem(x + m // 4, 4), lax.rem(z + lax.rem(m, 4), 4)

    def chain_at(x, z, cls, u):
        return xor4(xor4(cls, phase_key(u)), 2 * lax.rem(x + z, 2))

    def chain_of(u):
        return chain_at(x, z, cls, u)

    barrier = pltpu.get_barrier_semaphore()

    def greet(s, _):
        pl.semaphore_signal(barrier, inc=1, device_id=(lax.rem(me + s, DEVS), lat), device_id_type=MESH)
        return 0

    load_rows = pltpu.make_async_copy(rows_hbm, rowb.at[pl.ds(0, NLON // 8)], load_sem.at[0])
    load_wrap = pltpu.make_async_copy(rows_hbm.at[pl.ds(0, 12)], rowb.at[pl.ds(NLON // 8, 12)], load_sem.at[7])
    load_rows.start()
    load_wrap.start()
    lax.fori_loop(1, DEVS, greet, 0)
    pl.semaphore_signal(barrier, inc=1, device_id=other_lat, device_id_type=MESH)
    load_rows.wait()
    load_wrap.wait()
    shift = shift_ref[0]

    def cut(target):
        start = lax.rem(target * COLS + (NLON - 4) + shift, NLON)
        pieces[target] = slide(rowb, start, WIDE).astype(BF16)

    pl.semaphore_wait(barrier, DEVS)

    my_slot = 1 + me // 4

    def send_phase(u):
        def send(s, _):
            tx, tz = place(s)
            target = tx * 16 + tz * 4 + chain_at(tx, tz, cls, u)
            cut(target)

            @pl.when(target != me)
            def _():
                remote(pieces.at[target], chain.at[cls, my_slot], fwd_send, fwd_recv.at[cls], (target, lat)).start()

            @pl.when(target == me)
            def _():
                pltpu.make_async_copy(pieces.at[me], chain.at[cls, my_slot], self_sem.at[0]).start()

            return 0

        lax.fori_loop(0, ROWS, send, 0)

    send_phase(0)

    load_w_in = pltpu.make_async_copy(w_in_hbm, w_in, load_sem.at[1])
    load_w_out = pltpu.make_async_copy(w_out_hbm, w_out, load_sem.at[2])
    load_w_in.start()
    load_w_out.start()
    for q in range(CHAINS):
        pltpu.make_async_copy(cot_hbm.at[:, q], cotv.at[q], load_sem.at[3 + q]).start()

    no_row = 17 * lat
    for q in range(CHAINS):
        chain[q, no_row] = jnp.zeros((WIDE, C), BF16)

    def zero_gdp(r, _):
        for b in range(2):
            gdp[b, r] = jnp.zeros((WIDE + 8, C), F32)
        return 0

    lax.fori_loop(0, ROWS + 2, zero_gdp, 0)

    def zero_gw(r, _):
        for g in range(2):
            gw[g, pl.ds(pl.multiple_of(r * 16, 16), 16)] = jnp.zeros((16, FF), F32)
        return 0

    lax.fori_loop(0, 16, zero_gw, 0)

    edge = ROWS - (ROWS - 1) * lat
    beside = 17 * (1 - lat)

    def halo_copy(q):
        return remote(chain.at[q, edge], chain.at[q, 17 * lat], halo_send.at[q], halo_recv.at[q], other_lat)

    def halo_arrived(q):
        remote(chain.at[q, edge], chain.at[q, beside], halo_send.at[q], halo_recv.at[q], other_lat).wait_recv()

    def arrive(u):
        q = chain_of(u)

        @pl.when(q == cls)
        def _():
            some = chain.at[q, pl.ds(1, ROWS - 1)]
            remote(some, some, fwd_send, fwd_recv.at[q], other_lat).wait_recv()
            pltpu.make_async_copy(pieces.at[me], chain.at[cls, my_slot], self_sem.at[0]).wait()

        @pl.when(q != cls)
        def _():
            some = chain.at[q, pl.ds(1, ROWS)]
            remote(some, some, fwd_send, fwd_recv.at[q], other_lat).wait_recv()

        halo_copy(q).start()

    arrive(0)
    send_phase(1)
    load_w_in.wait()
    load_w_out.wait()
    for q in range(CHAINS):
        pltpu.make_async_copy(cot_hbm.at[:, q], cotv.at[q], load_sem.at[3 + q]).wait()

    def forward(q):
        def to_wide(r, _):
            wide[r] = chain[q, r].astype(F32)
            return 0

        lax.fori_loop(0, ROWS + 2, to_wide, 0)

        def row(t, _):
            depth = None
            for a in range(3):
                for b in range(3):
                    term = taps[3 * a + b : 3 * a + b + 1, :] * wide[t + a, 4 * b : 4 * b + COLS, :]
                    depth = term if depth is None else depth + term
            mean = jnp.mean(depth, axis=-1, keepdims=True)
            centred = depth - mean
            r = lax.rsqrt(jnp.mean(centred * centred, axis=-1, keepdims=True) + EPS)
            n = centred * r
            nhat[t] = n
            rinv[t] = jnp.broadcast_to(r, (COLS, 128))
            normed[t] = n.astype(BF16)
            return 0

        lax.fori_loop(0, ROWS, row, 0, unroll=2)

    def mlp(q):
        def step(h, _):
            at = pl.ds(h * STEP_ROWS, STEP_ROWS)
            nb = normed[at].reshape(CHUNK, C)
            cb = cotv[q, at].reshape(CHUNK, C)
            nbt = nb.T
            cbt = cb.T
            mlp_out = None
            g_norm = None
            for f in range(FF // 256):
                cols = slice(256 * f, 256 * f + 256)
                hid = dot(nb, w_in[:, cols])
                g_act = dot_t(cb, w_out[cols, :])
                h2 = hid * hid
                t = jnp.tanh(hid * (GELU_C + (GELU_C * GELU_A) * h2))
                p = 0.5 + 0.5 * t
                value = hid * p
                slope = p + value * (0.5 - 0.5 * t) * (2.0 * GELU_C + (6.0 * GELU_A * GELU_C) * h2)
                act = value.astype(BF16)
                g_hid = (g_act * slope).astype(BF16)
                out_part = dot(act, w_out[cols, :])
                norm_part = dot_t(g_hid, w_in[:, cols])
                mlp_out = out_part if mlp_out is None else mlp_out + out_part
                g_norm = norm_part if g_norm is None else g_norm + norm_part
                gw[0, :, cols] += dot(nbt, g_hid)
                gw[1, :, cols] += dot(cbt, act)
            gn[at] = g_norm.reshape(STEP_ROWS, COLS, C)
            centre = wide[pl.ds(1 + h * STEP_ROWS, STEP_ROWS), 4 : 4 + COLS, :]
            outv[q, at] = (centre + mlp_out.reshape(STEP_ROWS, COLS, C)).astype(BF16)
            return 0

        lax.fori_loop(0, ROWS // STEP_ROWS, step, 0)
        pltpu.make_async_copy(outv.at[q], out_hbm.at[:, q], out_sem.at[q]).start()

    def norm_back(q, buf, sums):
        def row(t, sums):
            n = nhat[t]
            g = gn[t]
            g_mean = jnp.mean(g, axis=-1, keepdims=True)
            g_proj = jnp.mean(g * n, axis=-1, keepdims=True)
            g_dw = (rinv[t][:, :1] * (g - g_mean - n * g_proj)).astype(BF16)
            wide_g = g_dw.astype(F32)
            gdp[buf, t + 1, 8 : 8 + COLS, :] = wide_g
            new = []
            for a in range(3):
                for b in range(3):
                    prod = wide[t + a, 4 * b : 4 * b + COLS, :] * wide_g
                    new.append(sums[3 * a + b] + jnp.sum(prod.reshape(COLS // 8, 8, C), axis=0))
            return tuple(new)

        sums = lax.fori_loop(0, ROWS, row, sums, unroll=2)
        ghalo_s[q] = gdp[buf, edge, 8 : 8 + COLS, :].astype(BF16)
        return sums

    def ghalo_copy(q):
        return remote(ghalo_s.at[q], ghalo_r.at[q], gh_send.at[q], gh_recv.at[q], other_lat)

    def back_row(q, buf, target):
        t = target // 4
        acc = None
        for a in range(3):
            for b in range(3):
                term = taps[3 * a + b : 3 * a + b + 1, :] * gdp[buf, t + 2 - a, 8 - 4 * b : 8 - 4 * b + WIDE, :]
                acc = term if acc is None else acc + term
        strip[...] = acc
        strip[4 : 4 + COLS, :] = strip[4 : 4 + COLS, :] + cotv[q, t].astype(F32)
        back_pieces[target] = strip[...].astype(BF16)

    def conv_back(q, buf):
        remote(ghalo_s.at[q], ghalo_r.at[q], gh_send.at[q], gh_recv.at[q], other_lat).wait_recv()
        gdp[buf, beside, 8 : 8 + COLS, :] = ghalo_r[q].astype(F32)

        def send(s, _):
            tx, tz = place(s)
            target = tx * 16 + tz * 4 + q
            back_row(q, buf, target)

            @pl.when(target != me)
            def _():
                remote(back_pieces.at[target], back_hbm.at[me], bwd_send, bwd_recv, (target, lat)).start()

            @pl.when(target == me)
            def _():
                pltpu.make_async_copy(back_pieces.at[me], back_hbm.at[me], self_sem.at[1]).start()

            return 0

        lax.fori_loop(0, ROWS, send, 0)

    def chain_step(u, sums):
        q = chain_of(u)
        buf = lax.rem(u, 2)
        halo_arrived(q)
        forward(q)

        @pl.when(u > 0)
        def _():
            conv_back(chain_of(u - 1), 1 - buf)

        @pl.when(u == 0)
        def _():
            send_phase(2)

        mlp(q)
        arrive(u + 1)
        sums = norm_back(q, buf, sums)
        ghalo_copy(q).start()

        @pl.when(u == 0)
        def _():
            send_phase(3)

        return sums

    last = CHAINS - 1
    sums = lax.fori_loop(0, last, chain_step, tuple(jnp.zeros((8, C), F32) for _ in range(9)))
    q = chain_of(last)
    halo_arrived(q)
    forward(q)
    conv_back(chain_of(last - 1), (last - 1) % 2)
    mlp(q)

    def halve(r, _):
        gsend[r] = gw[1 - core, pl.ds(pl.multiple_of(r * 8, 8), 8), :].astype(BF16)
        return 0

    lax.fori_loop(0, 32, halve, 0)
    core_copy = remote(gsend, grecv, core_send, core_recv, other_core)
    core_copy.start()

    sums = norm_back(q, last % 2, sums)
    ghalo_copy(q).start()
    for j in range(9):
        gk_mine[j : j + 1, :] = jnp.sum(sums[j], axis=0, keepdims=True)
    gk_lat_copy = remote(gk_mine, gk_lat, gkl_ssem, gkl_rsem, other_lat)
    gk_lat_copy.start()

    core_copy.wait()

    def pair(r, _):
        s = gw[core, pl.ds(pl.multiple_of(r * 8, 8), 8), :] + grecv[r].astype(F32)
        rs_send[r] = s.astype(BF16)
        return 0

    lax.fori_loop(0, 32, pair, 0)

    def chip_peer(s):
        m = lax.rem(11 * s, 32)
        yh = lax.rem(chip + m, 2)
        xz = lax.rem(chip // 2 + m // 2, 16)
        return xz * 2 + yh

    def rs_go(s, _):
        p = chip_peer(s)
        remote(rs_send.at[p], rs_recv.at[chip], rs_ssem, rs_rsem, (2 * p + core, lat)).start()
        return 0

    lax.fori_loop(1, 32, rs_go, 0)

    places = (x, z, cls)

    def gk_device(stage, other):
        at = [other if stage == n else places[n] for n in range(3)]
        return (at[0] * 16 + at[1] * 4 + at[2], lat)

    def gk_start(stage, value):
        mine = places[stage]
        gk_all[stage, mine] = value
        for n in range(1, 4):
            slot = gk_all.at[stage, mine]
            remote(slot, slot, gka_ssem.at[stage], gka_rsem.at[stage], gk_device(stage, lax.rem(mine + n, 4))).start()

    def gk_end(stage):
        some = gk_all.at[stage, pl.ds(0, 3)]
        remote(some, some, gka_ssem.at[stage], gka_rsem.at[stage], other_lat).wait()
        return (gk_all[stage, 0] + gk_all[stage, 1]) + (gk_all[stage, 2] + gk_all[stage, 3])

    conv_back(q, last % 2)
    gk_lat_copy.wait()
    gk_start(0, gk_mine[...] + gk_lat[...])

    rs_all = rs_send.at[pl.ds(1, 31)]
    remote(rs_all, rs_recv.at[pl.ds(1, 31)], rs_ssem, rs_rsem, other_lat).wait()
    rs_recv[chip] = rs_send[chip]

    def rs_sum(r, s):
        return s + rs_recv[r].astype(F32)

    lat_send[...] = lax.fori_loop(0, 32, rs_sum, jnp.zeros((8, FF), F32))
    lat_copy = remote(lat_send, lat_recv, lat_ssem, lat_rsem, other_lat)
    lat_copy.start()
    gk_start(1, gk_end(0))
    lat_copy.wait()
    ag[core, chip] = (lat_send[...] + lat_recv[...]).astype(BF16)

    def ag_go(s, _):
        p = chip_peer(s)
        remote(ag.at[core, chip], ag.at[core, chip], ag_ssem, ag_rsem, (2 * p + core, lat)).start()
        return 0

    lax.fori_loop(1, 32, ag_go, 0)
    gk_start(2, gk_end(1))
    ag_all = ag.at[core, pl.ds(1, 31)]
    remote(ag_all, ag_all, ag_ssem, ag_rsem, other_lat).wait()
    full = remote(ag.at[core], ag.at[core], full_ssem, full_rsem, other_core)
    full.start()
    save_mine = pltpu.make_async_copy(ag.at[core], grads_out.at[core], self_sem.at[2])
    save_mine.start()
    gk_out[...] = gk_end(2)
    full.wait()
    save_other = pltpu.make_async_copy(ag.at[1 - core], grads_out.at[1 - core], self_sem.at[3])
    save_other.start()

    pltpu.make_async_copy(back_pieces.at[me], back_hbm.at[me], self_sem.at[1]).wait()
    for q in range(CHAINS):
        halo_copy(q).wait_send()
        ghalo_copy(q).wait_send()
        pltpu.make_async_copy(outv.at[q], out_hbm.at[:, q], out_sem.at[q]).wait()
    fwd_rest = pieces.at[pl.ds(1, DEVS - 1)]
    remote(fwd_rest, fwd_rest, fwd_send, fwd_recv.at[0], other_lat).wait_send()
    back_rest = back_hbm.at[pl.ds(1, DEVS - 1)]
    remote(back_pieces.at[pl.ds(1, DEVS - 1)], back_rest, bwd_send, bwd_recv, other_lat).wait()
    save_mine.wait()
    save_other.wait()


def finish_kernel(
    shift_ref, scale, back, out_tmp, grads, gk, rows_ref, out_ref, gwi_ref, gwo_ref, gk_ref,
    backv, gradv, gkv, rowsv, outv, gwiv, gwov, full, in_sem, out_sem, sem,
):
    groups = 8
    each = DEVS // groups
    span = 256

    def load(g):
        at = pl.ds(g * each, each)
        return pltpu.make_async_copy(back.at[at], backv.at[at], in_sem.at[g])

    for g in range(groups):
        load(g).start()
    load_grads = pltpu.make_async_copy(grads, gradv, sem.at[0])
    load_grads.start()
    load_gk = pltpu.make_async_copy(gk, gkv, sem.at[1])
    load_gk.start()
    take_out = pltpu.make_async_copy(out_tmp, outv, sem.at[2])
    take_out.start()
    full[0] = jnp.zeros((8, C), F32)
    for g in range(groups):
        load(g).wait()

        def gather(n, _):
            j = g * each + n
            piece = backv[j].astype(F32).reshape(9, 8, C)
            full[8 * j] += piece[0]
            full[pl.ds(8 * j + 1, 8)] = piece[1:]
            return 0

        lax.fori_loop(0, each, gather, 0)
    take_out.wait()
    give_out = pltpu.make_async_copy(outv, out_ref, sem.at[2])
    give_out.start()
    seam = full[0] + full[NLON // 8]
    full[0] = seam
    full[NLON // 8] = seam
    full[NLON // 8 + 1 : NLON // 8 + 2 + span // 8] = full[1 : 2 + span // 8]
    shift = shift_ref[0]

    def emit_copy(r):
        at = pl.ds(pl.multiple_of(r * span, span), span)
        return pltpu.make_async_copy(rowsv.at[at], rows_ref.at[at], out_sem)

    def emit(r, _):
        start = lax.rem(r * span + NLON - shift, NLON) + 4
        first = lax.div(start, 8)
        off = start - 8 * first
        tiles = full[pl.ds(first, span // 8 + 1)]
        moved = pltpu.roll(tiles, lax.rem(8 - off, 8), 1)
        stays = lax.broadcasted_iota(jnp.int32, (span // 8, 8, C), 1) < 8 - off
        rows = jnp.where(stays, moved[:-1], moved[1:]).reshape(span, C)
        rowsv[pl.ds(pl.multiple_of(r * span, span), span), :] = rows.astype(BF16)
        emit_copy(r).start()
        return 0

    lax.fori_loop(0, NLON // span, emit, 0)
    load_grads.wait()
    gwiv[...] = scale * gradv[0].reshape(C, FF).astype(F32)
    store_i = pltpu.make_async_copy(gwiv, gwi_ref, sem.at[3])
    store_i.start()
    gwov[...] = (scale * gradv[1].reshape(C, FF).astype(F32)).T
    store_o = pltpu.make_async_copy(gwov, gwo_ref, sem.at[4])
    store_o.start()
    load_gk.wait()
    gk_ref[...] = scale * gkv[:9]
    pltpu.make_async_copy(rowsv, rows_ref, out_sem).wait()
    store_i.wait()
    store_o.wait()
    give_out.wait()


def shards(rows_in, row_shift, kernel, w_in, w_out, cotangent):
    hbm = pl.BlockSpec(memory_space=pltpu.HBM)
    vmem = pl.BlockSpec(memory_space=pltpu.VMEM)
    smem = pl.BlockSpec(memory_space=pltpu.SMEM)
    dma = pltpu.SemaphoreType.DMA
    v = pltpu.VMEM
    out_tmp, back, grads, gk = pl.pallas_call(
        block_kernel,
        out_shape=(
            jax.ShapeDtypeStruct((ROWS, CHAINS, COLS, C), BF16),
            jax.ShapeDtypeStruct((DEVS, WIDE, C), BF16),
            jax.ShapeDtypeStruct((2, 32, 8, FF), BF16),
            jax.ShapeDtypeStruct((16, C), F32),
        ),
        in_specs=[smem, hbm, vmem, hbm, hbm, hbm],
        out_specs=(hbm, hbm, hbm, vmem),
        scratch_shapes=[
            v((NLON // 8 + 12, 8, C), BF16), v((DEVS, WIDE, C), BF16), v((DEVS, WIDE, C), BF16),
            v((CHAINS, ROWS + 2, WIDE, C), BF16), v((CHAINS, ROWS, COLS, C), BF16),
            v((C, FF), BF16), v((FF, C), BF16), v((ROWS + 2, WIDE, C), F32),
            v((ROWS, COLS, C), F32), v((ROWS, COLS, 128), F32), v((ROWS, COLS, C), BF16),
            v((ROWS, COLS, C), F32), v((2, ROWS + 2, WIDE + 8, C), F32),
            v((CHAINS, COLS, C), BF16), v((CHAINS, COLS, C), BF16), v((WIDE, C), F32),
            v((CHAINS, ROWS, COLS, C), BF16), v((2, C, FF), F32),
            v((32, 8, FF), BF16), v((32, 8, FF), BF16), v((32, 8, FF), BF16), v((32, 8, FF), BF16),
            v((8, FF), F32), v((8, FF), F32), v((2, 32, 8, FF), BF16),
            v((16, C), F32), v((16, C), F32), v((3, 4, 16, C), F32),
            dma((8,)), dma, dma((4,)), dma((4,)), dma((4,)), dma((4,)), dma((4,)), dma, dma, dma((4,)), dma((4,)),
            dma, dma, dma, dma, dma, dma, dma, dma, dma, dma, dma, dma, dma((3,)), dma((3,)),
        ],
        compiler_params=pltpu.CompilerParams(
            collective_id=0, has_side_effects=True, vmem_limit_bytes=58 << 20
        ),
        name="block",
    )(row_shift, rows_in.reshape(NLON // 8, 8, C), kernel, w_in, w_out, cotangent.reshape(ROWS, CHAINS, COLS, C))
    scale = 1.0 / math.sqrt(2 * DEVS * NLON)
    rows, out, grad_in, grad_out, grad_kernel = pl.pallas_call(
        lambda shift_ref, *refs: finish_kernel(shift_ref, scale, *refs),
        out_shape=(
            jax.ShapeDtypeStruct((NLON, C), BF16),
            jax.ShapeDtypeStruct((ROWS, CHAINS, COLS, C), BF16),
            jax.ShapeDtypeStruct((C, FF), F32),
            jax.ShapeDtypeStruct((FF, C), F32),
            jax.ShapeDtypeStruct((9, C), F32),
        ),
        in_specs=[smem, hbm, hbm, hbm, hbm],
        out_specs=(hbm, hbm, hbm, hbm, vmem),
        scratch_shapes=[
            v((DEVS, WIDE, C), BF16), v((2, 32, 8, FF), BF16), v((16, C), F32), v((NLON, C), BF16),
            v((ROWS, CHAINS, COLS, C), BF16), v((C, FF), F32), v((FF, C), F32), v((NLON // 8 + 34, 8, C), F32), dma((8,)), dma, dma((5,)),
        ],
        compiler_params=pltpu.CompilerParams(vmem_limit_bytes=58 << 20),
        name="finish",
    )(row_shift, back, out_tmp, grads, gk)
    return (
        out.reshape(ROWS * CHAINS, COLS, C),
        rows[None],
        grad_kernel,
        grad_in,
        grad_out,
    )


def solution(mesh):
    in_specs = (
        P(("lat", "lon"), None, None),
        P(("lat", "lon")),
        P(),
        P(),
        P(),
        P("lat", "lon", None),
    )
    out_specs = (P("lat", "lon", None), P(("lat", "lon"), None, None), P(), P(), P())
    return jax.shard_map(shards, mesh=mesh, in_specs=in_specs, out_specs=out_specs, check_vma=False)
```

```python
import functools
import math

import jax
import jax.numpy as jnp
from jax import lax
from jax.experimental import pallas as pl
from jax.experimental.pallas import tpu as pltpu
from jax.sharding import PartitionSpec as P

MESH = pl.DeviceIdType.MESH
GELU_C = math.sqrt(2.0 / math.pi)
GELU_A = 0.044715
EPS = 1e-06
F32 = jnp.float32
BF16 = jnp.bfloat16

NLON = 4096
C = 256
FF = 1024
DEVS = 64
CHAINS = 4
ROWS = 16
COLS = 64
WIDE = COLS + 8
CHUNK = 1024
STEP_ROWS = CHUNK // COLS


def dot(a, b):
    return jnp.dot(a, b, preferred_element_type=F32)


def dot_t(a, b):
    return lax.dot_general(a, b, (((1,), (1,)), ((), ())), preferred_element_type=F32)


def xor4(a, b):
    return lax.rem(a + b, 2) + 2 * lax.rem(a // 2 + b // 2, 2)


def slide(ref, start, rows):
    first = lax.div(start, 8)
    off = start - 8 * first
    tiles = ref[pl.ds(first, rows // 8 + 3)].astype(F32)
    for by in (4, 2, 1):
        count = tiles.shape[0] - 1
        place = lax.broadcasted_iota(jnp.int32, (count, 8, C), 1)
        moved = pltpu.roll(tiles, 8 - by, 1)
        bit = jnp.full((count, 8, C), lax.rem(lax.div(off, by), 2), jnp.int32)
        tiles = jnp.where(bit == 1, jnp.where(place < 8 - by, moved[:-1], moved[1:]), tiles[:-1])
    return tiles.reshape(rows, C)


def phase_key(u):
    return 2 * lax.rem(u + u // 2, 2) + u // 2


def block_kernel(
    shift_ref, rows_hbm, taps, w_in_hbm, w_out_hbm, cot_hbm,
    out_hbm, back_hbm, grads_out, gk_out,
    rowb, pieces, back_pieces, chain, cotv, w_in, w_out, wide, nhat, rinv, normed, gn, gdp, ghalo_s, ghalo_r,
    strip, outv, gw, gsend, grecv, rs_send, rs_recv, lat_send, lat_recv, ag, gk_mine, gk_lat, gk_all,
    load_sem, fwd_send, fwd_recv, halo_send, halo_recv, gh_send, gh_recv, bwd_send, bwd_recv, out_sem, self_sem,
    core_send, core_recv, rs_ssem, rs_rsem, lat_ssem, lat_rsem, ag_ssem, ag_rsem, full_ssem, full_rsem,
    gkl_ssem, gkl_rsem, gka_ssem, gka_rsem,
):
    me = lax.axis_index("lon")
    lat = lax.axis_index("lat")
    x = me // 16
    z = lax.rem(me // 4, 4)
    cls = lax.rem(me, 4)
    core = lax.rem(me, 2)
    chip = me // 2
    other_lat = (me, 1 - lat)
    other_core = (me + 1 - 2 * core, lat)

    def remote(src, dst, ssem, rsem, device):
        return pltpu.make_async_remote_copy(
            src_ref=src, dst_ref=dst, send_sem=ssem, recv_sem=rsem, device_id=device, device_id_type=MESH
        )

    def place(s):
        m = lax.rem(5 * s, 16)
        return lax.rem(x + m // 4, 4), lax.rem(z + lax.rem(m, 4), 4)

    def chain_at(x, z, cls, u):
        return xor4(xor4(cls, phase_key(u)), 2 * lax.rem(x + z, 2))

    def chain_of(u):
        return chain_at(x, z, cls, u)

    barrier = pltpu.get_barrier_semaphore()

    def greet(s, _):
        pl.semaphore_signal(barrier, inc=1, device_id=(lax.rem(me + s, DEVS), lat), device_id_type=MESH)
        return 0

    load_rows = pltpu.make_async_copy(rows_hbm, rowb.at[pl.ds(0, NLON // 8)], load_sem.at[0])
    load_wrap = pltpu.make_async_copy(rows_hbm.at[pl.ds(0, 12)], rowb.at[pl.ds(NLON // 8, 12)], load_sem.at[7])
    load_rows.start()
    load_wrap.start()
    lax.fori_loop(1, DEVS, greet, 0)
    pl.semaphore_signal(barrier, inc=1, device_id=other_lat, device_id_type=MESH)
    load_rows.wait()
    load_wrap.wait()
    shift = shift_ref[0]

    def cut(target):
        start = lax.rem(target * COLS + (NLON - 4) + shift, NLON)
        pieces[target] = slide(rowb, start, WIDE).astype(BF16)

    pl.semaphore_wait(barrier, DEVS)

    my_slot = 1 + me // 4

    def send_phase(u):
        def send(s, _):
            tx, tz = place(s)
            target = tx * 16 + tz * 4 + chain_at(tx, tz, cls, u)
            cut(target)

            @pl.when(target != me)
            def _():
                remote(pieces.at[target], chain.at[cls, my_slot], fwd_send, fwd_recv.at[cls], (target, lat)).start()

            @pl.when(target == me)
            def _():
                pltpu.make_async_copy(pieces.at[me], chain.at[cls, my_slot], self_sem.at[0]).start()

            return 0

        lax.fori_loop(0, ROWS, send, 0)

    send_phase(0)

    load_w_in = pltpu.make_async_copy(w_in_hbm, w_in, load_sem.at[1])
    load_w_out = pltpu.make_async_copy(w_out_hbm, w_out, load_sem.at[2])
    load_w_in.start()
    load_w_out.start()
    for q in range(CHAINS):
        pltpu.make_async_copy(cot_hbm.at[:, q], cotv.at[q], load_sem.at[3 + q]).start()

    no_row = 17 * lat
    for q in range(CHAINS):
        chain[q, no_row] = jnp.zeros((WIDE, C), BF16)

    def zero_gdp(r, _):
        for b in range(2):
            gdp[b, r] = jnp.zeros((WIDE + 8, C), F32)
        return 0

    lax.fori_loop(0, ROWS + 2, zero_gdp, 0)

    def zero_gw(r, _):
        for g in range(2):
            gw[g, pl.ds(pl.multiple_of(r * 16, 16), 16)] = jnp.zeros((16, FF), F32)
        return 0

    lax.fori_loop(0, 16, zero_gw, 0)

    edge = ROWS - (ROWS - 1) * lat
    beside = 17 * (1 - lat)

    def halo_copy(q):
        return remote(chain.at[q, edge], chain.at[q, 17 * lat], halo_send.at[q], halo_recv.at[q], other_lat)

    def halo_arrived(q):
        remote(chain.at[q, edge], chain.at[q, beside], halo_send.at[q], halo_recv.at[q], other_lat).wait_recv()

    def arrive(u):
        q = chain_of(u)

        @pl.when(q == cls)
        def _():
            some = chain.at[q, pl.ds(1, ROWS - 1)]
            remote(some, some, fwd_send, fwd_recv.at[q], other_lat).wait_recv()
            pltpu.make_async_copy(pieces.at[me], chain.at[cls, my_slot], self_sem.at[0]).wait()

        @pl.when(q != cls)
        def _():
            some = chain.at[q, pl.ds(1, ROWS)]
            remote(some, some, fwd_send, fwd_recv.at[q], other_lat).wait_recv()

        halo_copy(q).start()

    arrive(0)
    send_phase(1)
    load_w_in.wait()
    load_w_out.wait()
    for q in range(CHAINS):
        pltpu.make_async_copy(cot_hbm.at[:, q], cotv.at[q], load_sem.at[3 + q]).wait()

    def forward(q):
        def to_wide(r, _):
            wide[r] = chain[q, r].astype(F32)
            return 0

        lax.fori_loop(0, ROWS + 2, to_wide, 0)

        def row(t, _):
            depth = None
            for a in range(3):
                for b in range(3):
                    term = taps[3 * a + b : 3 * a + b + 1, :] * wide[t + a, 4 * b : 4 * b + COLS, :]
                    depth = term if depth is None else depth + term
            mean = jnp.mean(depth, axis=-1, keepdims=True)
            centred = depth - mean
            r = lax.rsqrt(jnp.mean(centred * centred, axis=-1, keepdims=True) + EPS)
            n = centred * r
            nhat[t] = n
            rinv[t] = jnp.broadcast_to(r, (COLS, 128))
            normed[t] = n.astype(BF16)
            return 0

        lax.fori_loop(0, ROWS, row, 0, unroll=2)

    def mlp(q):
        def step(h, _):
            at = pl.ds(h * STEP_ROWS, STEP_ROWS)
            nb = normed[at].reshape(CHUNK, C)
            cb = cotv[q, at].reshape(CHUNK, C)
            nbt = nb.T
            cbt = cb.T
            mlp_out = None
            g_norm = None
            for f in range(FF // 256):
                cols = slice(256 * f, 256 * f + 256)
                hid = dot(nb, w_in[:, cols])
                g_act = dot_t(cb, w_out[cols, :])
                h2 = hid * hid
                t = jnp.tanh(hid * (GELU_C + (GELU_C * GELU_A) * h2))
                p = 0.5 + 0.5 * t
                value = hid * p
                slope = p + value * (0.5 - 0.5 * t) * (2.0 * GELU_C + (6.0 * GELU_A * GELU_C) * h2)
                act = value.astype(BF16)
                g_hid = (g_act * slope).astype(BF16)
                out_part = dot(act, w_out[cols, :])
                norm_part = dot_t(g_hid, w_in[:, cols])
                mlp_out = out_part if mlp_out is None else mlp_out + out_part
                g_norm = norm_part if g_norm is None else g_norm + norm_part
                gw[0, :, cols] += dot(nbt, g_hid)
                gw[1, :, cols] += dot(cbt, act)
            gn[at] = g_norm.reshape(STEP_ROWS, COLS, C)
            centre = wide[pl.ds(1 + h * STEP_ROWS, STEP_ROWS), 4 : 4 + COLS, :]
            outv[q, at] = (centre + mlp_out.reshape(STEP_ROWS, COLS, C)).astype(BF16)
            return 0

        lax.fori_loop(0, ROWS // STEP_ROWS, step, 0)
        pltpu.make_async_copy(outv.at[q], out_hbm.at[:, q], out_sem.at[q]).start()

    def norm_back(q, buf, sums):
        def row(t, sums):
            n = nhat[t]
            g = gn[t]
            g_mean = jnp.mean(g, axis=-1, keepdims=True)
            g_proj = jnp.mean(g * n, axis=-1, keepdims=True)
            g_dw = (rinv[t][:, :1] * (g - g_mean - n * g_proj)).astype(BF16)
            wide_g = g_dw.astype(F32)
            gdp[buf, t + 1, 8 : 8 + COLS, :] = wide_g
            new = []
            for a in range(3):
                for b in range(3):
                    prod = wide[t + a, 4 * b : 4 * b + COLS, :] * wide_g
                    new.append(sums[3 * a + b] + jnp.sum(prod.reshape(COLS // 8, 8, C), axis=0))
            return tuple(new)

        sums = lax.fori_loop(0, ROWS, row, sums, unroll=2)
        ghalo_s[q] = gdp[buf, edge, 8 : 8 + COLS, :].astype(BF16)
        return sums

    def ghalo_copy(q):
        return remote(ghalo_s.at[q], ghalo_r.at[q], gh_send.at[q], gh_recv.at[q], other_lat)

    def back_row(q, buf, target):
        t = target // 4
        acc = None
        for a in range(3):
            for b in range(3):
                term = taps[3 * a + b : 3 * a + b + 1, :] * gdp[buf, t + 2 - a, 8 - 4 * b : 8 - 4 * b + WIDE, :]
                acc = term if acc is None else acc + term
        strip[...] = acc
        strip[4 : 4 + COLS, :] = strip[4 : 4 + COLS, :] + cotv[q, t].astype(F32)
        back_pieces[target] = strip[...].astype(BF16)

    def conv_back(q, buf):
        remote(ghalo_s.at[q], ghalo_r.at[q], gh_send.at[q], gh_recv.at[q], other_lat).wait_recv()
        gdp[buf, beside, 8 : 8 + COLS, :] = ghalo_r[q].astype(F32)

        def send(s, _):
            tx, tz = place(s)
            target = tx * 16 + tz * 4 + q
            back_row(q, buf, target)

            @pl.when(target != me)
            def _():
                remote(back_pieces.at[target], back_hbm.at[me], bwd_send, bwd_recv, (target, lat)).start()

            @pl.when(target == me)
            def _():
                pltpu.make_async_copy(back_pieces.at[me], back_hbm.at[me], self_sem.at[1]).start()

            return 0

        lax.fori_loop(0, ROWS, send, 0)

    def chain_step(u, sums):
        q = chain_of(u)
        buf = lax.rem(u, 2)
        halo_arrived(q)
        forward(q)

        @pl.when(u > 0)
        def _():
            conv_back(chain_of(u - 1), 1 - buf)

        @pl.when(u == 0)
        def _():
            send_phase(2)

        mlp(q)
        arrive(u + 1)
        sums = norm_back(q, buf, sums)
        ghalo_copy(q).start()

        @pl.when(u == 0)
        def _():
            send_phase(3)

        return sums

    last = CHAINS - 1
    sums = lax.fori_loop(0, last, chain_step, tuple(jnp.zeros((8, C), F32) for _ in range(9)))
    q = chain_of(last)
    halo_arrived(q)
    forward(q)
    conv_back(chain_of(last - 1), (last - 1) % 2)
    mlp(q)

    def halve(r, _):
        gsend[r] = gw[1 - core, pl.ds(pl.multiple_of(r * 8, 8), 8), :].astype(BF16)
        return 0

    lax.fori_loop(0, 32, halve, 0)
    core_copy = remote(gsend, grecv, core_send, core_recv, other_core)
    core_copy.start()

    sums = norm_back(q, last % 2, sums)
    ghalo_copy(q).start()
    for j in range(9):
        gk_mine[j : j + 1, :] = jnp.sum(sums[j], axis=0, keepdims=True)
    gk_lat_copy = remote(gk_mine, gk_lat, gkl_ssem, gkl_rsem, other_lat)
    gk_lat_copy.start()

    core_copy.wait()

    def pair(r, _):
        s = gw[core, pl.ds(pl.multiple_of(r * 8, 8), 8), :] + grecv[r].astype(F32)
        rs_send[r] = s.astype(BF16)
        return 0

    lax.fori_loop(0, 32, pair, 0)

    def chip_peer(s):
        m = lax.rem(11 * s, 32)
        yh = lax.rem(chip + m, 2)
        xz = lax.rem(chip // 2 + m // 2, 16)
        return xz * 2 + yh

    def rs_go(s, _):
        p = chip_peer(s)
        remote(rs_send.at[p], rs_recv.at[chip], rs_ssem, rs_rsem, (2 * p + core, lat)).start()
        return 0

    lax.fori_loop(1, 32, rs_go, 0)

    places = (x, z, cls)

    def gk_device(stage, other):
        at = [other if stage == n else places[n] for n in range(3)]
        return (at[0] * 16 + at[1] * 4 + at[2], lat)

    def gk_start(stage, value):
        mine = places[stage]
        gk_all[stage, mine] = value
        for n in range(1, 4):
            slot = gk_all.at[stage, mine]
            remote(slot, slot, gka_ssem.at[stage], gka_rsem.at[stage], gk_device(stage, lax.rem(mine + n, 4))).start()

    def gk_end(stage):
        some = gk_all.at[stage, pl.ds(0, 3)]
        remote(some, some, gka_ssem.at[stage], gka_rsem.at[stage], other_lat).wait()
        return (gk_all[stage, 0] + gk_all[stage, 1]) + (gk_all[stage, 2] + gk_all[stage, 3])

    conv_back(q, last % 2)
    gk_lat_copy.wait()
    gk_start(0, gk_mine[...] + gk_lat[...])

    rs_all = rs_send.at[pl.ds(1, 31)]
    remote(rs_all, rs_recv.at[pl.ds(1, 31)], rs_ssem, rs_rsem, other_lat).wait()
    rs_recv[chip] = rs_send[chip]

    def rs_sum(r, s):
        return s + rs_recv[r].astype(F32)

    lat_send[...] = lax.fori_loop(0, 32, rs_sum, jnp.zeros((8, FF), F32))
    lat_copy = remote(lat_send, lat_recv, lat_ssem, lat_rsem, other_lat)
    lat_copy.start()
    gk_start(1, gk_end(0))
    lat_copy.wait()
    ag[core, chip] = (lat_send[...] + lat_recv[...]).astype(BF16)

    def ag_go(s, _):
        p = chip_peer(s)
        remote(ag.at[core, chip], ag.at[core, chip], ag_ssem, ag_rsem, (2 * p + core, lat)).start()
        return 0

    lax.fori_loop(1, 32, ag_go, 0)
    gk_start(2, gk_end(1))
    ag_all = ag.at[core, pl.ds(1, 31)]
    remote(ag_all, ag_all, ag_ssem, ag_rsem, other_lat).wait()
    full = remote(ag.at[core], ag.at[core], full_ssem, full_rsem, other_core)
    full.start()
    save_mine = pltpu.make_async_copy(ag.at[core], grads_out.at[core], self_sem.at[2])
    save_mine.start()
    gk_out[...] = gk_end(2)
    full.wait()
    save_other = pltpu.make_async_copy(ag.at[1 - core], grads_out.at[1 - core], self_sem.at[3])
    save_other.start()

    pltpu.make_async_copy(back_pieces.at[me], back_hbm.at[me], self_sem.at[1]).wait()
    for q in range(CHAINS):
        halo_copy(q).wait_send()
        ghalo_copy(q).wait_send()
        pltpu.make_async_copy(outv.at[q], out_hbm.at[:, q], out_sem.at[q]).wait()
    fwd_rest = pieces.at[pl.ds(1, DEVS - 1)]
    remote(fwd_rest, fwd_rest, fwd_send, fwd_recv.at[0], other_lat).wait_send()
    back_rest = back_hbm.at[pl.ds(1, DEVS - 1)]
    remote(back_pieces.at[pl.ds(1, DEVS - 1)], back_rest, bwd_send, bwd_recv, other_lat).wait()
    save_mine.wait()
    save_other.wait()


def finish_kernel(
    shift_ref, scale, back, out_tmp, grads, gk, rows_ref, out_ref, gwi_ref, gwo_ref, gk_ref,
    backv, gradv, gkv, rowsv, outv, gwiv, gwov, full, in_sem, out_sem, sem,
):
    groups = 8
    each = DEVS // groups
    span = 256

    def load(g):
        at = pl.ds(g * each, each)
        return pltpu.make_async_copy(back.at[at], backv.at[at], in_sem.at[g])

    for g in range(groups):
        load(g).start()
    load_grads = pltpu.make_async_copy(grads, gradv, sem.at[0])
    load_grads.start()
    load_gk = pltpu.make_async_copy(gk, gkv, sem.at[1])
    load_gk.start()
    take_out = pltpu.make_async_copy(out_tmp, outv, sem.at[2])
    take_out.start()
    full[0] = jnp.zeros((8, C), F32)
    for g in range(groups):
        load(g).wait()

        def gather(n, _):
            j = g * each + n
            piece = backv[j].astype(F32).reshape(9, 8, C)
            full[8 * j] += piece[0]
            full[pl.ds(8 * j + 1, 8)] = piece[1:]
            return 0

        lax.fori_loop(0, each, gather, 0)
    take_out.wait()
    give_out = pltpu.make_async_copy(outv, out_ref, sem.at[2])
    give_out.start()
    seam = full[0] + full[NLON // 8]
    full[0] = seam
    full[NLON // 8] = seam
    full[NLON // 8 + 1 : NLON // 8 + 2 + span // 8] = full[1 : 2 + span // 8]
    shift = shift_ref[0]

    def emit_copy(r):
        at = pl.ds(pl.multiple_of(r * span, span), span)
        return pltpu.make_async_copy(rowsv.at[at], rows_ref.at[at], out_sem)

    def emit(r, _):
        start = lax.rem(r * span + NLON - shift, NLON) + 4
        first = lax.div(start, 8)
        off = start - 8 * first
        tiles = full[pl.ds(first, span // 8 + 1)]
        moved = pltpu.roll(tiles, lax.rem(8 - off, 8), 1)
        stays = lax.broadcasted_iota(jnp.int32, (span // 8, 8, C), 1) < 8 - off
        rows = jnp.where(stays, moved[:-1], moved[1:]).reshape(span, C)
        rowsv[pl.ds(pl.multiple_of(r * span, span), span), :] = rows.astype(BF16)
        emit_copy(r).start()
        return 0

    lax.fori_loop(0, NLON // span, emit, 0)
    load_grads.wait()
    gwiv[...] = scale * gradv[0].reshape(C, FF).astype(F32)
    store_i = pltpu.make_async_copy(gwiv, gwi_ref, sem.at[3])
    store_i.start()
    gwov[...] = (scale * gradv[1].reshape(C, FF).astype(F32)).T
    store_o = pltpu.make_async_copy(gwov, gwo_ref, sem.at[4])
    store_o.start()
    load_gk.wait()
    gk_ref[...] = scale * gkv[:9]
    pltpu.make_async_copy(rowsv, rows_ref, out_sem).wait()
    store_i.wait()
    store_o.wait()
    give_out.wait()


def shards(rows_in, row_shift, kernel, w_in, w_out, cotangent):
    hbm = pl.BlockSpec(memory_space=pltpu.HBM)
    vmem = pl.BlockSpec(memory_space=pltpu.VMEM)
    smem = pl.BlockSpec(memory_space=pltpu.SMEM)
    dma = pltpu.SemaphoreType.DMA
    v = pltpu.VMEM
    out_tmp, back, grads, gk = pl.pallas_call(
        block_kernel,
        out_shape=(
            jax.ShapeDtypeStruct((ROWS, CHAINS, COLS, C), BF16),
            jax.ShapeDtypeStruct((DEVS, WIDE, C), BF16),
            jax.ShapeDtypeStruct((2, 32, 8, FF), BF16),
            jax.ShapeDtypeStruct((16, C), F32),
        ),
        in_specs=[smem, hbm, vmem, hbm, hbm, hbm],
        out_specs=(hbm, hbm, hbm, vmem),
        scratch_shapes=[
            v((NLON // 8 + 12, 8, C), BF16), v((DEVS, WIDE, C), BF16), v((DEVS, WIDE, C), BF16),
            v((CHAINS, ROWS + 2, WIDE, C), BF16), v((CHAINS, ROWS, COLS, C), BF16),
            v((C, FF), BF16), v((FF, C), BF16), v((ROWS + 2, WIDE, C), F32),
            v((ROWS, COLS, C), F32), v((ROWS, COLS, 128), F32), v((ROWS, COLS, C), BF16),
            v((ROWS, COLS, C), F32), v((2, ROWS + 2, WIDE + 8, C), F32),
            v((CHAINS, COLS, C), BF16), v((CHAINS, COLS, C), BF16), v((WIDE, C), F32),
            v((CHAINS, ROWS, COLS, C), BF16), v((2, C, FF), F32),
            v((32, 8, FF), BF16), v((32, 8, FF), BF16), v((32, 8, FF), BF16), v((32, 8, FF), BF16),
            v((8, FF), F32), v((8, FF), F32), v((2, 32, 8, FF), BF16),
            v((16, C), F32), v((16, C), F32), v((3, 4, 16, C), F32),
            dma((8,)), dma, dma((4,)), dma((4,)), dma((4,)), dma((4,)), dma((4,)), dma, dma, dma((4,)), dma((4,)),
            dma, dma, dma, dma, dma, dma, dma, dma, dma, dma, dma, dma, dma((3,)), dma((3,)),
        ],
        compiler_params=pltpu.CompilerParams(
            collective_id=0, has_side_effects=True, vmem_limit_bytes=58 << 20
        ),
        name="block",
    )(row_shift, rows_in.reshape(NLON // 8, 8, C), kernel, w_in, w_out, cotangent.reshape(ROWS, CHAINS, COLS, C))
    scale = 1.0 / math.sqrt(2 * DEVS * NLON)
    rows, out, grad_in, grad_out, grad_kernel = pl.pallas_call(
        lambda shift_ref, *refs: finish_kernel(shift_ref, scale, *refs),
        out_shape=(
            jax.ShapeDtypeStruct((NLON, C), BF16),
            jax.ShapeDtypeStruct((ROWS, CHAINS, COLS, C), BF16),
            jax.ShapeDtypeStruct((C, FF), F32),
            jax.ShapeDtypeStruct((FF, C), F32),
            jax.ShapeDtypeStruct((9, C), F32),
        ),
        in_specs=[smem, hbm, hbm, hbm, hbm],
        out_specs=(hbm, hbm, hbm, hbm, vmem),
        scratch_shapes=[
            v((DEVS, WIDE, C), BF16), v((2, 32, 8, FF), BF16), v((16, C), F32), v((NLON, C), BF16),
            v((ROWS, CHAINS, COLS, C), BF16), v((C, FF), F32), v((FF, C), F32), v((NLON // 8 + 34, 8, C), F32), dma((8,)), dma, dma((5,)),
        ],
        compiler_params=pltpu.CompilerParams(vmem_limit_bytes=58 << 20),
        name="finish",
    )(row_shift, back, out_tmp, grads, gk)
    return (
        out.reshape(ROWS * CHAINS, COLS, C),
        rows[None],
        grad_kernel,
        grad_in,
        grad_out,
    )


def solution(mesh):
    in_specs = (
        P(("lat", "lon"), None, None),
        P(("lat", "lon")),
        P(),
        P(),
        P(),
        P("lat", "lon", None),
    )
    out_specs = (P("lat", "lon", None), P(("lat", "lon"), None, None), P(), P(), P())
    return jax.shard_map(shards, mesh=mesh, in_specs=in_specs, out_specs=out_specs, check_vma=False)
```
